32 devices in a mesh: task: 16 (over z, x, core), tensor: 2 (over y).
Axes of the slice: x: 2, y: 2, z: 4, core: 2. Of those that a mesh axis runs over, the one named last changes fastest.
Arguments:
- inputs: bfloat16 [3072, 8192], P('task'), may hold values from -6 to 6
- queries: bfloat16 [3072, 4096], P('task', 'tensor'), may hold values from -6 to 6
- task_vectors: bfloat16 [8, 2, 8192, 1024], P(None, None, 'task', 'tensor'), may hold values from -0.0625 to 0.0625
- base_weights: bfloat16 [2, 8192, 1024], P(None, 'task', 'tensor'), may hold values from -0.0625 to 0.0625
- scale_exps: int32 [8, 2, 64, 8], P(None, None, 'task', 'tensor'), may hold values from -3 to 0
- coefs: float32 [8, 2], replicated, may hold values from 0.1 to 0.6
Outputs:
- attended: bfloat16 [3072, 4096], P('task', 'tensor')
- mean_entropy: float32 [], replicated
- coef_grad: float32 [8, 2], replicated
The draws below stay inside these ranges and needn't reach their ends.
All inputs are finite; a program needn't handle non-finite values.
Results may differ from the reference program's by a relative error of at most 0.0087.
Values may be sent and summed in bfloat16 or wider, within the bound.
A program may use at most 128 MiB of HBM per device.

```python
import math
import jax
import jax.numpy as jnp

D = 8192
HEAD = 128
KVH = 8
GROUP = 4
TASKS = 8
BLOCK = 128
TOK_DEV = 192
TOKENS = 3072
KVW = 1024
QW = 4096


def plant(result, stream_key, smallest, high):
    dims = result.shape
    index_at = [jax.random.randint(jax.random.fold_in(stream_key, axis), (), 0, dims[axis]) for axis in range(len(dims))]
    result = result.at[tuple(index_at)].set(smallest)
    longest = dims.index(max(dims))
    index_at[longest] = (index_at[longest] + 1) % dims[longest]
    return result.at[tuple(index_at)].set(high)


def block_levels(stream_key, shape, cuts, least, high):
    factor_of, own = 1.0, jax.random.fold_in(stream_key, 6)
    for axis_at, blocks in cuts:
        steps = jnp.exp(jax.random.uniform(jax.random.fold_in(own, axis_at), (blocks,), jnp.float32, least / len(cuts), high / len(cuts)))
        factor_of = factor_of * jnp.repeat(steps, shape[axis_at] // blocks).reshape([-1 if axis == axis_at else 1 for axis in range(len(shape))])
    return factor_of


def scatter_about(stream_key, extent, width, most, split=(), held_as=jnp.bfloat16):
    result = width * jax.random.normal(stream_key, extent, jnp.float32)
    if split:
        result = result * block_levels(stream_key, extent, split, -0.22, 0.18)
    return jnp.clip(result, -most, most).astype(held_as)


def setup_inputs(seed: int = 0) -> dict:
    key_list = jax.random.split(jax.random.key(seed), 7)
    inputs = scatter_about(key_list[0], (TOKENS, D), 1.0, 6.0, ((0, 16),))
    queries = scatter_about(key_list[1], (TOKENS, QW), 1.0, 6.0, ((0, 16), (1, 2)))
    task_vectors = scatter_about(key_list[2], (TASKS, 2, D, KVW), D ** -0.5, 0.0625, ((2, 16), (3, 2)))
    base_weights = scatter_about(key_list[3], (2, D, KVW), D ** -0.5, 0.0625, ((1, 16), (2, 2)))
    scale_exps = plant(jax.random.randint(key_list[4], (TASKS, 2, D // BLOCK, KVW // BLOCK), -3, 1), jax.random.fold_in(key_list[4], 1), -3, 0).astype(jnp.int32)
    coefs = jnp.clip(jnp.exp(jax.random.uniform(key_list[5], (TASKS, 2), jnp.float32, math.log(0.1), math.log(0.6))), 0.1, 0.6)
    return {"inputs": inputs, "queries": queries, "task_vectors": task_vectors, "base_weights": base_weights, "scale_exps": scale_exps, "coefs": coefs}


sharpen = 4.0
capping = 8.0
masked_value = -1e30


def dequantize(vectors, exponents):
    tasks, mats, rows, cols = vectors.shape
    row_blocks = exponents.shape[2]
    col_blocks = exponents.shape[3]
    factor = jnp.exp2(exponents.astype(jnp.float32))
    blocked = vectors.astype(jnp.float32).reshape(tasks, mats, row_blocks, rows // row_blocks, col_blocks, cols // col_blocks)
    blocked = blocked * factor[:, :, :, None, :, None]
    return blocked.reshape(tasks, mats, rows, cols)


def reference(inputs, queries, task_vectors, base_weights, scale_exps, coefs):
    scaled = dequantize(task_vectors, scale_exps)
    merged = (base_weights.astype(jnp.float32) + jnp.sum(coefs[:, :, None, None] * scaled, axis=0)).astype(jnp.bfloat16)
    keys_b = jnp.dot(inputs, merged[0], preferred_element_type=jnp.float32).astype(jnp.bfloat16)
    values_b = jnp.dot(inputs, merged[1], preferred_element_type=jnp.float32).astype(jnp.bfloat16)
    nseq = TOKENS // TOK_DEV
    query_all = queries.astype(jnp.float32).reshape(nseq, TOK_DEV, KVH, GROUP, HEAD)
    key_all = keys_b.astype(jnp.float32).reshape(nseq, TOK_DEV, KVH, HEAD)
    value_all = values_b.astype(jnp.float32).reshape(nseq, TOK_DEV, KVH, HEAD)
    inverse = HEAD ** -0.5
    scores = jnp.einsum('nshrd,nthd->nhrst', query_all, key_all) * inverse
    position = jnp.arange(TOK_DEV)
    causal = position[None, :] <= position[:, None]
    scores = jnp.where(causal, scores, masked_value)
    probs = jax.nn.softmax(scores, axis=-1)
    probs_b = probs.astype(jnp.bfloat16)
    outputs = jnp.einsum('nhrst,nthd->nshrd', probs_b.astype(jnp.float32), value_all)
    attended = outputs.astype(jnp.bfloat16).reshape(TOKENS, QW)
    logits = capping * jnp.tanh(sharpen * attended.astype(jnp.float32) / capping)
    expo = jnp.exp(logits)
    total = jnp.sum(expo, axis=1, keepdims=True)
    moment = jnp.sum(expo * logits, axis=1, keepdims=True)
    entropy = jnp.log(total[:, 0]) - moment[:, 0] / total[:, 0]
    mean_entropy = jnp.sum(entropy) / TOKENS
    slope = sharpen * (1.0 - (logits / capping) ** 2)
    d_out = (slope * (-(expo / total) * (logits - moment / total))).astype(jnp.bfloat16)
    d_out_f = d_out.astype(jnp.float32).reshape(nseq, TOK_DEV, KVH, GROUP, HEAD)
    d_probs = jnp.einsum('nshrd,nthd->nhrst', d_out_f, value_all)
    d_scores = (probs * (d_probs - jnp.sum(probs * d_probs, axis=-1, keepdims=True))).astype(jnp.bfloat16)
    d_keys = jnp.einsum('nhrst,nshrd->nthd', d_scores.astype(jnp.float32), query_all) * inverse
    d_values = jnp.einsum('nhrst,nshrd->nthd', probs_b.astype(jnp.float32), d_out_f)
    d_keys_b = d_keys.astype(jnp.bfloat16).reshape(TOKENS, KVW)
    d_values_b = d_values.astype(jnp.bfloat16).reshape(TOKENS, KVW)
    grad_keys = jnp.dot(inputs.T, d_keys_b, preferred_element_type=jnp.float32)
    grad_values = jnp.dot(inputs.T, d_values_b, preferred_element_type=jnp.float32)
    weight_grads = jnp.stack([grad_keys, grad_values])
    coef_grad = jnp.sum(weight_grads[None] * scaled, axis=(2, 3))
    return attended, mean_entropy, coef_grad
```

```python
import functools
import math

import jax
import jax.numpy as jnp
from jax import lax
from jax.experimental import pallas as pl
from jax.experimental.pallas import tpu as pltpu
from jax.sharding import PartitionSpec as P

HEAD = 128
GROUP = 4

sharpen = 4.0
capping = 8.0
masked_value = -1e30

MESH = pl.DeviceIdType.MESH
VMEM_BYTES = 60 * 1024 * 1024
F32 = jnp.float32
BF16 = jnp.bfloat16


def factors(n_task):
    outer = math.gcd(n_task, 4)
    mid = math.gcd(n_task // outer, 2)
    return outer, mid, n_task // (outer * mid)


def place(dims):
    _, mid, inner = dims
    task = lax.axis_index("task")
    rest = lax.rem(task, mid * inner)
    return task, task // (mid * inner), rest // inner, lax.rem(rest, inner)


def turned(value, step, size):
    return lax.rem(value + (step + size), size)


def index_of(dims, a, b, c):
    _, mid, inner = dims
    return (a * mid + b) * inner + c


def meet(peers):
    sem = pltpu.get_barrier_semaphore()
    for peer in peers:
        pl.semaphore_signal(sem, inc=1, device_id=peer, device_id_type=MESH)
    pl.semaphore_wait(sem, len(peers))


def send(src, dst, send_sem, recv_sem, peer):
    copy = pltpu.make_async_remote_copy(
        src_ref=src,
        dst_ref=dst,
        send_sem=send_sem,
        recv_sem=recv_sem,
        device_id=peer,
        device_id_type=MESH,
    )
    copy.start()
    return copy


def fetch(src, dst, sem):
    copy = pltpu.make_async_copy(src, dst, sem)
    copy.start()
    return copy


def project_kernel(
    dims, n_tensor, row_blocks, col_blocks,
    inputs, vectors, base, scales,
    kv_out, rows_out,
    xin, mg, vec_v, base_v, acc, pout, pin,
    local_sem, keep_sem, x_send, x_recv, y_send, y_recv, g_send, g_recv, r_send, r_recv, p_send, p_recv,
):
    outer, mid, inner = dims
    group = mid * inner
    task, a, b, c = place(dims)
    y = lax.axis_index("tensor")
    mine = b * inner + c
    tasks, mats, rows, cols = vectors.shape
    span = group * rows
    part = span // n_tensor

    def at(a_, b_, c_):
        return {"task": index_of(dims, a_, b_, c_), "tensor": y}

    def tensor_peer(step):
        return {"task": task, "tensor": turned(y, step, n_tensor)}

    def group_peer(f, e):
        return at(a, turned(b, f, mid), turned(c, e, inner))

    peers = [at(turned(a, d, outer), b, c) for d in range(1, outer)]
    peers += [group_peer(f, e) for f in range(mid) for e in range(inner) if f or e]
    peers += [tensor_peer(s) for s in range(1, n_tensor)]
    vec_copy = fetch(vectors, vec_v, local_sem.at[0])
    base_copy = fetch(base, base_v, local_sem.at[1])
    own_copy = fetch(
        inputs.at[:, pl.ds(pl.multiple_of(a * span, 128), span)], xin.at[a], local_sem.at[2]
    )
    meet(peers)
    sent = []
    x_copies = {}
    own_cols = pl.ds(pl.multiple_of(y * part, 128), part)
    for d in range(1, outer):
        to = turned(a, d, outer)
        x_copies[d] = send(
            inputs.at[:, pl.ds(pl.multiple_of(to * span + y * part, 128), part)],
            xin.at[a, :, own_cols],
            x_send.at[d], x_recv.at[d], at(to, b, c),
        )
        sent.append(x_copies[d])
    base_copy.wait()
    vec_copy.wait()
    high = rows // row_blocks
    wide = cols // col_blocks

    def merge(step, carry):
        m = step // row_blocks
        i = lax.rem(step, row_blocks)
        these = pl.ds(pl.multiple_of(i * high, 8), high)
        for j in range(col_blocks):
            across = slice(j * wide, (j + 1) * wide)
            total = base_v[m, these, across].astype(F32)
            for t in range(tasks):
                scale = scales[((t * mats + m) * row_blocks + i) * col_blocks + j]
                total += scale * vec_v[t, m, these, across].astype(F32)
            mg[mine, m, these, across] = total.astype(BF16)
        return carry

    lax.fori_loop(0, mats * row_blocks, merge, 0)

    g_copies = {}
    for f in range(1, mid):
        g_copies[f, 0] = send(
            mg.at[mine], mg.at[mine], g_send.at[f * inner], g_recv.at[f * inner], group_peer(f, 0)
        )
    for e in range(1, inner):
        g_copies[0, e] = send(mg.at[mine], mg.at[mine], g_send.at[e], g_recv.at[e], group_peer(0, e))
    y_copies = {}

    def pass_on(d):
        x_copies[d].wait_recv()
        block = xin.at[turned(a, -d, outer), :, own_cols]
        for s in range(1, n_tensor):
            slot = d * n_tensor + s
            y_copies[d, s] = send(block, block, y_send.at[slot], y_recv.at[slot], tensor_peer(s))
            sent.append(y_copies[d, s])

    for f in range(1, mid):
        g_copies[f, 0].wait_recv()
        came = turned(b, -f, mid) * inner + c
        for e in range(1, inner):
            slot = f * inner + e
            g_copies[f, e] = send(
                mg.at[came], mg.at[came], g_send.at[slot], g_recv.at[slot], group_peer(0, e)
            )
    sent.extend(g_copies.values())

    def spread(d):
        a_from = turned(a, -d, outer)
        owner = a_from * group + mine
        for f in range(mid):
            for e in range(inner):
                if not (f or e):
                    continue
                to = turned(b, f, mid) * inner + turned(c, e, inner)
                slot = (d * mid + f) * inner + e
                r_copies.append(
                    send(
                        xin.at[a_from, :, pl.ds(pl.multiple_of(to * rows, 128), rows)],
                        rows_out.at[owner],
                        r_send.at[slot], r_recv.at[slot], group_peer(f, e),
                    )
                )
        keeps.append(
            fetch(
                xin.at[a_from, :, pl.ds(pl.multiple_of(mine * rows, 128), rows)],
                rows_out.at[owner],
                keep_sem.at[d],
            )
        )

    def product(d, m):
        a_from = turned(a, -d, outer)
        total = None
        for k in range(group):
            term = jnp.dot(
                xin[a_from, :, k * rows:(k + 1) * rows], mg[k, m], preferred_element_type=F32
            )
            total = term if total is None else total + term
        return total

    r_copies = []
    keeps = []
    own_copy.wait()
    spread(0)
    for f in range(mid):
        for e in range(1, inner):
            g_copies[f, e].wait_recv()
    for m in range(mats):
        acc[m] = product(0, m)
    p_copies = []
    if outer > 1:
        pass_on(1)
    for d in range(1, outer):
        if d + 1 < outer:
            pass_on(d + 1)
        for s in range(1, n_tensor):
            y_copies[d, s].wait_recv()
        for m in range(mats):
            pout[d, m] = product(d, m).astype(BF16)
        p_copies.append(
            send(pout.at[d], pin.at[d], p_send.at[d], p_recv.at[d], at(turned(a, -d, outer), b, c))
        )
        spread(d)
    for d, copy in enumerate(p_copies, 1):
        copy.wait_recv()
        for m in range(mats):
            acc[m] += pin[d, m].astype(F32)
    for m in range(mats):
        kv_out[m] = acc[m].astype(BF16)
    for copy in keeps:
        copy.wait()
    for copy in r_copies:
        copy.wait_recv()
    for copy in sent + p_copies + r_copies:
        copy.wait_send()


def project(dims, n_tensor, inputs, vectors, base, scales, blocks):
    outer, mid, inner = dims
    group = mid * inner
    tokens = inputs.shape[0]
    _, mats, rows, cols = vectors.shape
    span = group * rows
    dma = pltpu.SemaphoreType.DMA
    count = outer * group
    return pl.pallas_call(
        functools.partial(project_kernel, dims, n_tensor, *blocks),
        out_shape=(
            jax.ShapeDtypeStruct((mats, tokens, cols), BF16),
            jax.ShapeDtypeStruct((count, tokens, rows), BF16),
        ),
        in_specs=[
            pl.BlockSpec(memory_space=pl.ANY),
            pl.BlockSpec(memory_space=pl.ANY),
            pl.BlockSpec(memory_space=pl.ANY),
            pl.BlockSpec(memory_space=pltpu.SMEM),
        ],
        out_specs=(pl.BlockSpec(memory_space=pltpu.VMEM), pl.BlockSpec(memory_space=pl.ANY)),
        scratch_shapes=[
            pltpu.VMEM((outer, tokens, span), BF16),
            pltpu.VMEM((group, mats, rows, cols), BF16),
            pltpu.VMEM(vectors.shape, BF16),
            pltpu.VMEM(base.shape, BF16),
            pltpu.VMEM((mats, tokens, cols), F32),
            pltpu.VMEM((outer, mats, tokens, cols), BF16),
            pltpu.VMEM((outer, mats, tokens, cols), BF16),
            dma((3,)), dma((outer,)),
            dma((outer,)), dma((outer,)),
            dma((outer * n_tensor,)), dma((outer * n_tensor,)),
            dma((group,)), dma((group,)),
            dma((count,)), dma((count,)),
            dma((outer,)), dma((outer,)),
        ],
        compiler_params=pltpu.CompilerParams(
            collective_id=0, has_side_effects=True, vmem_limit_bytes=VMEM_BYTES
        ),
        name="project",
    )(inputs, vectors, base, scales)


def attend_kernel(
    n_tensor, queries, kv, att_out, dkv_out, ent_out, probs, logs, expos, sums, s_send, s_recv
):
    task = lax.axis_index("task")
    y = lax.axis_index("tensor")
    tokens = queries.shape[0]
    heads = kv.shape[2] // HEAD
    inverse = HEAD ** (-0.5)
    peers = [{"task": task, "tensor": turned(y, s, n_tensor)} for s in range(1, n_tensor)]
    if peers:
        meet(peers)
    key_at = lax.broadcasted_iota(jnp.int32, (tokens, GROUP * tokens), 0)
    query_at = lax.rem(lax.broadcasted_iota(jnp.int32, (tokens, GROUP * tokens), 1), tokens)
    causal = key_at <= query_at

    def stacked(h):
        return jnp.concatenate(
            [queries[:, (h * GROUP + r) * HEAD:(h * GROUP + r + 1) * HEAD] for r in range(GROUP)],
            axis=0,
        )

    total = jnp.zeros((tokens, HEAD), F32)
    moment = jnp.zeros((tokens, HEAD), F32)
    for h in range(heads):
        cut = slice(h * HEAD, (h + 1) * HEAD)
        scores = lax.dot_general(
            kv[0, :, cut], stacked(h), (((1,), (1,)), ((), ())), preferred_element_type=F32
        ) * inverse
        scores = jnp.where(causal, scores, masked_value)
        weight = jnp.exp(scores - jnp.max(scores, axis=0, keepdims=True))
        prob = weight * (1.0 / jnp.sum(weight, axis=0, keepdims=True))
        probs[h] = prob
        att = lax.dot_general(
            prob.astype(BF16), kv[1, :, cut], (((0,), (0,)), ((), ())), preferred_element_type=F32
        ).astype(BF16)
        logits = capping * jnp.tanh(sharpen * att.astype(F32) / capping)
        expo = jnp.exp(logits)
        logs[h] = logits
        expos[h] = expo
        scaled = expo * logits
        for r in range(GROUP):
            here = slice(r * tokens, (r + 1) * tokens)
            att_out[:, (h * GROUP + r) * HEAD:(h * GROUP + r + 1) * HEAD] = att[here]
            total += expo[here]
            moment += scaled[here]
    sums[y] = jnp.concatenate(
        [
            jnp.sum(total.T, axis=0, keepdims=True),
            jnp.sum(moment.T, axis=0, keepdims=True),
            jnp.zeros((6, tokens), F32),
        ],
        axis=0,
    )
    copies = [
        send(sums.at[y], sums.at[y], s_send.at[s], s_recv.at[s], peer)
        for s, peer in enumerate(peers)
    ]
    for copy in copies:
        copy.wait_recv()
    whole = sums[0]
    for s in range(1, n_tensor):
        whole = whole + sums[s]
    over = 1.0 / whole[0:1]
    average = whole[1:2] * over
    ent_out[...] = jnp.log(whole[0:1]) - average
    over_col = jnp.broadcast_to(over, (HEAD, tokens)).T
    average_col = jnp.broadcast_to(average, (HEAD, tokens)).T
    over_all = jnp.concatenate([over_col] * GROUP, axis=0)
    average_all = jnp.concatenate([average_col] * GROUP, axis=0)
    for h in range(heads):
        cut = slice(h * HEAD, (h + 1) * HEAD)
        logits = logs[h]
        slope = sharpen * (1.0 - (logits / capping) ** 2)
        d_out = (slope * (-(expos[h] * over_all) * (logits - average_all))).astype(BF16)
        prob = probs[h]
        d_probs = lax.dot_general(
            kv[1, :, cut], d_out, (((1,), (1,)), ((), ())), preferred_element_type=F32
        )
        d_scores = (
            prob * (d_probs - jnp.sum(prob * d_probs, axis=0, keepdims=True))
        ).astype(BF16)
        d_keys = jnp.dot(d_scores, stacked(h), preferred_element_type=F32) * inverse
        d_values = jnp.dot(prob.astype(BF16), d_out, preferred_element_type=F32)
        dkv_out[0, :, cut] = d_keys.astype(BF16)
        dkv_out[1, :, cut] = d_values.astype(BF16)
    for copy in copies:
        copy.wait_send()


def attend(n_tensor, queries, kv):
    tokens = queries.shape[0]
    heads = kv.shape[2] // HEAD
    vmem = pl.BlockSpec(memory_space=pltpu.VMEM)
    dma = pltpu.SemaphoreType.DMA
    return pl.pallas_call(
        functools.partial(attend_kernel, n_tensor),
        out_shape=(
            jax.ShapeDtypeStruct(queries.shape, BF16),
            jax.ShapeDtypeStruct(kv.shape, BF16),
            jax.ShapeDtypeStruct((1, tokens), F32),
        ),
        in_specs=[vmem, vmem],
        out_specs=(vmem, vmem, vmem),
        scratch_shapes=[
            pltpu.VMEM((heads, tokens, GROUP * tokens), F32),
            pltpu.VMEM((heads, GROUP * tokens, HEAD), F32),
            pltpu.VMEM((heads, GROUP * tokens, HEAD), F32),
            pltpu.VMEM((n_tensor, 8, tokens), F32),
            dma((n_tensor,)), dma((n_tensor,)),
        ],
        compiler_params=pltpu.CompilerParams(
            collective_id=1, has_side_effects=True, vmem_limit_bytes=VMEM_BYTES
        ),
        name="attend",
    )(queries, kv)


def reduce_kernel(
    dims, n_tensor, row_blocks, col_blocks,
    dkv, rows_in, vectors, factor, ent, out,
    got, rows_v, vec_v, grads, held, held_t,
    local_sem, g_send, g_recv, t_send, t_recv, y_send, y_recv,
):
    outer, mid, inner = dims
    n_task = outer * mid * inner
    task, a, b, c = place(dims)
    y = lax.axis_index("tensor")
    tasks, mats, rows, cols = vectors.shape

    rows_copy = fetch(rows_in, rows_v, local_sem.at[0])
    vec_copy = fetch(vectors, vec_v, local_sem.at[1])

    def to(d, f, e):
        spot = index_of(dims, turned(a, d, outer), turned(b, f, mid), turned(c, e, inner))
        return {"task": spot, "tensor": y}

    def source(d, f, e):
        return index_of(dims, turned(a, -d, outer), turned(b, -f, mid), turned(c, -e, inner))

    task_peers = [{"task": turned(task, s, n_task), "tensor": y} for s in range(1, n_task)]
    tensor_peers = [{"task": task, "tensor": turned(y, s, n_tensor)} for s in range(1, n_tensor)]
    meet(task_peers + tensor_peers)
    copies = {}

    def forward(held_at, hop):
        d, f, e = held_at
        where = source(d, f, e)
        slot = tuple(p + q for p, q in zip(held_at, hop))
        flat = (slot[0] * mid + slot[1]) * inner + slot[2]
        copies[slot] = send(
            got.at[where] if any(held_at) else dkv,
            got.at[where],
            g_send.at[flat], g_recv.at[flat], to(*hop),
        )

    def take(slot):
        if any(slot):
            copies[slot].wait_recv()
            block = got.at[source(*slot)]
        else:
            block = dkv
        d, f, e = slot
        if not e:
            if not f:
                for step in range(1, mid):
                    forward(slot, (0, step, 0))
            for step in range(1, inner):
                forward(slot, (0, 0, step))
        return block

    def gather(block, where, first):
        left = rows_v[where]
        for m in range(mats):
            term = lax.dot_general(
                left, block[m], (((0,), (0,)), ((), ())), preferred_element_type=F32
            )
            if first:
                grads[m] = term
            else:
                grads[m] += term

    for d in range(1, outer):
        forward((0, 0, 0), (d, 0, 0))
    rows_copy.wait()
    for step in range(outer + 2):
        slots = []
        if step < outer:
            slots.append((step, 0, 0))
        if 1 <= step <= outer:
            slots += [(step - 1, f, 0) for f in range(1, mid)]
            slots += [(step - 1, 0, e) for e in range(1, inner)]
        if step >= 2:
            slots += [(step - 2, f, e) for f in range(1, mid) for e in range(1, inner)]
        for slot in slots:
            gather(take(slot), source(*slot), not any(slot))
    vec_copy.wait()
    high = rows // row_blocks
    wide = cols // col_blocks
    lines = []
    for m in range(mats):
        def contract(i, carry):
            these = pl.ds(pl.multiple_of(i * high, 8), high)
            carry = list(carry)
            for j in range(col_blocks):
                across = slice(j * wide, (j + 1) * wide)
                grad = grads[m, these, across]
                for t in range(tasks):
                    scale = factor[((t * mats + m) * row_blocks + i) * col_blocks + j]
                    term = grad * vec_v[t, m, these, across].astype(F32)
                    term = jnp.sum(term.reshape(high // 8, 8, wide), axis=0)
                    carry[t] = carry[t] + scale * term
            return tuple(carry)

        start = tuple(jnp.zeros((8, wide), F32) for _ in range(tasks))
        lines.append(lax.fori_loop(0, row_blocks, contract, start))
    parts = [
        jnp.sum(lines[m][t], axis=0, keepdims=True) for t in range(tasks) for m in range(mats)
    ]
    entropy = jnp.broadcast_to(jnp.sum(ent[...]) / (n_tensor * wide), (1, wide))
    pad = held.shape[1] - len(parts) - 1
    held[task] = jnp.concatenate(parts + [entropy, jnp.zeros((pad, wide), F32)], axis=0)
    last = [
        send(held.at[task], held.at[task], t_send.at[s], t_recv.at[s], peer)
        for s, peer in enumerate(task_peers)
    ]
    for copy in last:
        copy.wait_recv()
    total = held[0]
    for k in range(1, n_task):
        total = total + held[k]
    held_t[y] = total
    more = [
        send(held_t.at[y], held_t.at[y], y_send.at[s], y_recv.at[s], peer)
        for s, peer in enumerate(tensor_peers)
    ]
    for copy in more:
        copy.wait_recv()
    total = held_t[0]
    for k in range(1, n_tensor):
        total = total + held_t[k]
    out[...] = jnp.sum(total, axis=1, keepdims=True)
    for copy in list(copies.values()) + last + more:
        copy.wait_send()


def reduce(dims, n_tensor, dkv, rows_in, vectors, factor, ent, blocks):
    n_task, tokens, rows = rows_in.shape
    tasks, mats, _, cols = vectors.shape
    wide = cols // blocks[1]
    lines = -(-(tasks * mats + 1) // 8) * 8
    vmem = pl.BlockSpec(memory_space=pltpu.VMEM)
    hbm = pl.BlockSpec(memory_space=pl.ANY)
    dma = pltpu.SemaphoreType.DMA
    return pl.pallas_call(
        functools.partial(reduce_kernel, dims, n_tensor, *blocks),
        out_shape=jax.ShapeDtypeStruct((lines, 1), F32),
        in_specs=[vmem, hbm, hbm, pl.BlockSpec(memory_space=pltpu.SMEM), vmem],
        out_specs=vmem,
        scratch_shapes=[
            pltpu.VMEM((n_task, mats, tokens, cols), BF16),
            pltpu.VMEM((n_task, tokens, rows), BF16),
            pltpu.VMEM(vectors.shape, BF16),
            pltpu.VMEM((mats, rows, cols), F32),
            pltpu.VMEM((n_task, lines, wide), F32),
            pltpu.VMEM((n_tensor, lines, wide), F32),
            dma((2,)),
            dma((n_task,)), dma((n_task,)),
            dma((n_task,)), dma((n_task,)),
            dma((n_tensor,)), dma((n_tensor,)),
        ],
        compiler_params=pltpu.CompilerParams(
            collective_id=2, has_side_effects=True, vmem_limit_bytes=VMEM_BYTES
        ),
        name="reduce",
    )(dkv, rows_in, vectors, factor, ent)


def local(inputs, queries, task_vectors, base_weights, scale_exps, coefs):
    n_task = lax.axis_size("task")
    n_tensor = lax.axis_size("tensor")
    dims = factors(n_task)
    tasks, mats = coefs.shape
    blocks = scale_exps.shape[2:]
    factor = jnp.exp2(scale_exps.astype(F32))
    scales = coefs[:, :, None, None] * factor
    kv, rows_in = project(
        dims, n_tensor, inputs, task_vectors, base_weights, scales.reshape(-1), blocks
    )
    attended, dkv, ent = attend(n_tensor, queries, kv)
    sums = reduce(dims, n_tensor, dkv, rows_in, task_vectors, factor.reshape(-1), ent, blocks)
    coef_grad = sums[: tasks * mats, 0].reshape(tasks, mats)
    mean_entropy = sums[tasks * mats, 0] / (inputs.shape[0] * n_task)
    return (attended, mean_entropy, coef_grad)


def solution(mesh):
    return jax.shard_map(
        local,
        mesh=mesh,
        in_specs=(
            P("task", None),
            P("task", "tensor"),
            P(None, None, "task", "tensor"),
            P(None, "task", "tensor"),
            P(None, None, "task", "tensor"),
            P(),
        ),
        out_specs=(P("task", "tensor"), P(), P()),
        check_vma=False,
    )
```

```python
import functools
import math

import jax
import jax.numpy as jnp
from jax import lax
from jax.experimental import pallas as pl
from jax.experimental.pallas import tpu as pltpu
from jax.sharding import PartitionSpec as P

HEAD = 128
GROUP = 4

sharpen = 4.0
capping = 8.0
masked_value = -1e30

MESH = pl.DeviceIdType.MESH
VMEM_BYTES = 60 * 1024 * 1024
F32 = jnp.float32
BF16 = jnp.bfloat16


def factors(n_task):
    outer = math.gcd(n_task, 4)
    mid = math.gcd(n_task // outer, 2)
    return outer, mid, n_task // (outer * mid)


def place(dims):
    _, mid, inner = dims
    task = lax.axis_index("task")
    rest = lax.rem(task, mid * inner)
    return task, task // (mid * inner), rest // inner, lax.rem(rest, inner)


def turned(value, step, size):
    return lax.rem(value + (step + size), size)


def flip(value, step):
    bit = 1
    for_value = value
    while bit <= step:
        if step & bit:
            for_value = for_value + bit - 2 * bit * lax.rem(value // bit, 2)
        bit *= 2
    return for_value


def scale_of(exps, t, m, i, j):
    return lax.shift_left(jnp.int32(1), exps[t, m, i, j] + 3).astype(F32) * 0.125


def index_of(dims, a, b, c):
    _, mid, inner = dims
    return (a * mid + b) * inner + c


def meet(peers):
    sem = pltpu.get_barrier_semaphore()
    for peer in peers:
        pl.semaphore_signal(sem, inc=1, device_id=peer, device_id_type=MESH)
    pl.semaphore_wait(sem, len(peers))


def send(src, dst, send_sem, recv_sem, peer):
    copy = pltpu.make_async_remote_copy(
        src_ref=src,
        dst_ref=dst,
        send_sem=send_sem,
        recv_sem=recv_sem,
        device_id=peer,
        device_id_type=MESH,
    )
    copy.start()
    return copy


def fetch(src, dst, sem):
    copy = pltpu.make_async_copy(src, dst, sem)
    copy.start()
    return copy


def project_kernel(
    dims, n_tensor, pieces,
    inputs, vectors, base, exps, coefs,
    kv_out, rows_out,
    xin, mg, vec_v, base_v, acc, hold, pout, pin,
    local_sem, keep_sem, x_send, x_recv, y_send, y_recv, g_send, g_recv, r_send, r_recv, p_send, p_recv,
):
    outer, mid, inner = dims
    group = mid * inner
    task, a, b, c = place(dims)
    y = lax.axis_index("tensor")
    mine = b * inner + c
    tasks, mats, rows, cols = vectors.shape
    row_blocks, col_blocks = exps.shape[2:]
    tokens = inputs.shape[0]
    piece = tokens // pieces
    span = group * rows
    part = span // n_tensor
    turns = list(range(outer - 1, 0, -1))

    def at(a_, b_, c_):
        return {"task": index_of(dims, a_, b_, c_), "tensor": y}

    def tensor_peer(step):
        return {"task": task, "tensor": turned(y, step, n_tensor)}

    def group_peer(f, e):
        return at(a, turned(b, f, mid), turned(c, e, inner))

    def some(k):
        return slice(k * piece, (k + 1) * piece)

    peers = [at(flip(a, d), b, c) for d in turns]
    peers += [group_peer(f, e) for f in range(mid) for e in range(inner) if f or e]
    peers += [tensor_peer(s) for s in range(1, n_tensor)]
    base_copy = fetch(base, base_v, local_sem.at[0])
    vec_copies = [
        fetch(vectors.at[:, m], vec_v.at[:, m], local_sem.at[2 + m]) for m in range(mats)
    ]
    own_copy = fetch(
        inputs.at[:, pl.ds(pl.multiple_of(a * span, 128), span)], xin.at[a], local_sem.at[1]
    )
    meet(peers)
    sent = []
    x_copies = {}
    own_cols = pl.ds(pl.multiple_of(y * part, 128), part)
    for k in range(pieces):
        for d in turns:
            to = flip(a, d)
            slot = d * pieces + k
            x_copies[k, d] = send(
                inputs.at[some(k), pl.ds(pl.multiple_of(to * span + y * part, 128), part)],
                xin.at[a, some(k), own_cols],
                x_send.at[slot], x_recv.at[slot], at(to, b, c),
            )
            sent.append(x_copies[k, d])
    high = rows // row_blocks
    wide = cols // col_blocks
    base_copy.wait()
    g_copies = {}

    def share(m, f, e, hop):
        came = turned(b, -(f - hop[0]), mid) * inner + turned(c, -(e - hop[1]), inner)
        slot = (m * mid + f) * inner + e
        g_copies[m, f, e] = send(
            mg.at[came, m], mg.at[came, m], g_send.at[slot], g_recv.at[slot], group_peer(*hop)
        )
        sent.append(g_copies[m, f, e])

    for m in range(mats):
        vec_copies[m].wait()

        def merge(i, carry):
            these = pl.ds(pl.multiple_of(i * high, 8), high)
            for j in range(col_blocks):
                across = slice(j * wide, (j + 1) * wide)
                total = base_v[m, these, across].astype(F32)
                for t in range(tasks):
                    scale = coefs[t, m] * scale_of(exps, t, m, i, j)
                    total += scale * vec_v[t, m, these, across].astype(F32)
                mg[mine, m, these, across] = total.astype(BF16)
            return carry

        lax.fori_loop(0, row_blocks, merge, 0)
        for f in range(1, mid):
            share(m, f, 0, (f, 0))
        for e in range(1, inner):
            share(m, 0, e, (0, e))

    r_copies = []
    keeps = []

    def spread(k, d):
        a_from = flip(a, d)
        owner = a_from * group + mine
        for f in range(mid):
            for e in range(inner):
                if not (f or e):
                    continue
                to = turned(b, f, mid) * inner + turned(c, e, inner)
                slot = ((k * outer + d) * mid + f) * inner + e
                r_copies.append(
                    send(
                        xin.at[a_from, some(k), pl.ds(pl.multiple_of(to * rows, 128), rows)],
                        rows_out.at[owner, some(k)],
                        r_send.at[slot], r_recv.at[slot], group_peer(f, e),
                    )
                )
        keeps.append(
            fetch(
                xin.at[a_from, some(k), pl.ds(pl.multiple_of(mine * rows, 128), rows)],
                rows_out.at[owner, some(k)],
                keep_sem.at[k * outer + d],
            )
        )

    y_copies = {}

    def pass_on(k):
        for d in turns:
            x_copies[k, d].wait_recv()
            block = xin.at[flip(a, d), some(k), own_cols]
            for s in range(1, n_tensor):
                slot = (k * outer + d) * n_tensor + s
                y_copies[k, d, s] = send(
                    block, block, y_send.at[slot], y_recv.at[slot], tensor_peer(s)
                )
                sent.append(y_copies[k, d, s])

    def share_on(m):
        for f in range(1, mid):
            g_copies[m, f, 0].wait_recv()
            for e in range(1, inner):
                share(m, f, e, (0, e))

    def own_part(m):
        for f in range(mid):
            for e in range(1, inner):
                g_copies[m, f, e].wait_recv()
        total = None
        for g in range(group):
            term = jnp.dot(
                xin[a, :, g * rows:(g + 1) * rows], mg[g, m], preferred_element_type=F32
            )
            total = term if total is None else total + term
        acc[m] = total

    p_copies = {}

    def give(k, m, d, to):
        slot = (d * pieces + k) * mats + m
        p_copies[k, m, d] = send(
            pout.at[d, m, some(k)], pin.at[d, m, some(k)],
            p_send.at[slot], p_recv.at[slot], at(flip(a, to), b, c),
        )
        sent.append(p_copies[k, m, d])

    def parts(k, m):
        if m == 0:
            for d in turns:
                for s in range(1, n_tensor):
                    y_copies[k, d, s].wait_recv()
        if not turns:
            return
        total = None
        for g in range(group):
            left = jnp.concatenate(
                [xin[flip(a, d), some(k), g * rows:(g + 1) * rows] for d in turns], axis=0
            )
            term = jnp.dot(left, mg[g, m], preferred_element_type=F32)
            total = term if total is None else total + term
        for n, d in enumerate(turns):
            mine_part = total[n * piece:(n + 1) * piece]
            if d == 2:
                hold[m, some(k)] = mine_part
            else:
                pout[d, m, some(k)] = mine_part.astype(BF16)
                give(k, m, d, 1)

    def combine(k, m):
        if 2 not in turns:
            return
        p_copies[k, m, 3].wait_recv()
        pout[2, m, some(k)] = (hold[m, some(k)] + pin[3, m, some(k)].astype(F32)).astype(BF16)
        give(k, m, 2, 2)

    last = pieces - 1
    pass_on(0)
    own_copy.wait()
    for k in range(pieces):
        spread(k, 0)
    share_on(0)
    for k in range(1, last):
        pass_on(k)
    own_part(0)
    for k in range(last):
        parts(k, 0)
        if k:
            combine(k - 1, 0)
    share_on(1)
    if last:
        pass_on(last)
        combine(last - 1, 0)
    parts(last, 0)
    own_part(1)
    parts(0, 1)
    combine(last, 0)
    for k in range(1, pieces):
        parts(k, 1)
        combine(k - 1, 1)
        for d in turns:
            spread(k - 1, d)
    combine(last, 1)
    for d in turns:
        spread(last, d)
    for m in range(mats):
        for k in range(pieces):
            total = acc[m, some(k)]
            for d in turns:
                if d < 3:
                    p_copies[k, m, d].wait_recv()
                    total = total + pin[d, m, some(k)].astype(F32)
            kv_out[m, some(k)] = total.astype(BF16)
    for copy in keeps:
        copy.wait()
    for copy in r_copies:
        copy.wait_recv()
    for copy in sent + r_copies:
        copy.wait_send()


def project(dims, n_tensor, inputs, vectors, base, exps, coefs):
    outer, mid, inner = dims
    group = mid * inner
    tokens = inputs.shape[0]
    _, mats, rows, cols = vectors.shape
    span = group * rows
    pieces = math.gcd(tokens // 16, 3)
    dma = pltpu.SemaphoreType.DMA
    count = outer * group
    hbm = pl.BlockSpec(memory_space=pl.ANY)
    smem = pl.BlockSpec(memory_space=pltpu.SMEM)
    return pl.pallas_call(
        functools.partial(project_kernel, dims, n_tensor, pieces),
        out_shape=(
            jax.ShapeDtypeStruct((mats, tokens, cols), BF16),
            jax.ShapeDtypeStruct((count, tokens, rows), BF16),
        ),
        in_specs=[hbm, hbm, hbm, smem, smem],
        out_specs=(pl.BlockSpec(memory_space=pltpu.VMEM), hbm),
        scratch_shapes=[
            pltpu.VMEM((outer, tokens, span), BF16),
            pltpu.VMEM((group, mats, rows, cols), BF16),
            pltpu.VMEM(vectors.shape, BF16),
            pltpu.VMEM(base.shape, BF16),
            pltpu.VMEM((mats, tokens, cols), F32),
            pltpu.VMEM((mats, tokens, cols), F32),
            pltpu.VMEM((outer, mats, tokens, cols), BF16),
            pltpu.VMEM((outer, mats, tokens, cols), BF16),
            dma((2 + mats,)), dma((pieces * outer,)),
            dma((outer * pieces,)), dma((outer * pieces,)),
            dma((pieces * outer * n_tensor,)), dma((pieces * outer * n_tensor,)),
            dma((mats * group,)), dma((mats * group,)),
            dma((pieces * count,)), dma((pieces * count,)),
            dma((outer * pieces * mats,)), dma((outer * pieces * mats,)),
        ],
        compiler_params=pltpu.CompilerParams(
            collective_id=0, has_side_effects=True, vmem_limit_bytes=VMEM_BYTES
        ),
        name="project",
    )(inputs, vectors, base, exps, coefs)


def attend_kernel(
    n_tensor, queries, kv, att_out, dkv_out, ent_out, probs, logs, expos, sums, s_send, s_recv
):
    task = lax.axis_index("task")
    y = lax.axis_index("tensor")
    tokens = queries.shape[0]
    heads = kv.shape[2] // HEAD
    inverse = HEAD ** (-0.5)
    peers = [{"task": task, "tensor": turned(y, s, n_tensor)} for s in range(1, n_tensor)]
    if peers:
        meet(peers)
    key_at = lax.broadcasted_iota(jnp.int32, (tokens, GROUP * tokens), 0)
    query_at = lax.rem(lax.broadcasted_iota(jnp.int32, (tokens, GROUP * tokens), 1), tokens)
    causal = key_at <= query_at

    def stacked(h):
        return jnp.concatenate(
            [queries[:, (h * GROUP + r) * HEAD:(h * GROUP + r + 1) * HEAD] for r in range(GROUP)],
            axis=0,
        )

    total = jnp.zeros((tokens, HEAD), F32)
    moment = jnp.zeros((tokens, HEAD), F32)
    for h in range(heads):
        cut = slice(h * HEAD, (h + 1) * HEAD)
        scores = lax.dot_general(
            kv[0, :, cut], stacked(h), (((1,), (1,)), ((), ())), preferred_element_type=F32
        ) * inverse
        scores = jnp.where(causal, scores, masked_value)
        weight = jnp.exp(scores - jnp.max(scores, axis=0, keepdims=True))
        prob = weight * (1.0 / jnp.sum(weight, axis=0, keepdims=True))
        probs[h] = prob
        att = lax.dot_general(
            prob.astype(BF16), kv[1, :, cut], (((0,), (0,)), ((), ())), preferred_element_type=F32
        ).astype(BF16)
        logits = capping * jnp.tanh(sharpen * att.astype(F32) / capping)
        expo = jnp.exp(logits)
        logs[h] = logits
        expos[h] = expo
        scaled = expo * logits
        for r in range(GROUP):
            here = slice(r * tokens, (r + 1) * tokens)
            att_out[:, (h * GROUP + r) * HEAD:(h * GROUP + r + 1) * HEAD] = att[here]
            total += expo[here]
            moment += scaled[here]
    sums[y] = jnp.concatenate(
        [
            jnp.sum(total.T, axis=0, keepdims=True),
            jnp.sum(moment.T, axis=0, keepdims=True),
            jnp.zeros((6, tokens), F32),
        ],
        axis=0,
    )
    copies = [
        send(sums.at[y], sums.at[y], s_send.at[s], s_recv.at[s], peer)
        for s, peer in enumerate(peers)
    ]
    for copy in copies:
        copy.wait_recv()
    whole = sums[0]
    for s in range(1, n_tensor):
        whole = whole + sums[s]
    over = 1.0 / whole[0:1]
    average = whole[1:2] * over
    ent_out[...] = jnp.log(whole[0:1]) - average
    over_col = jnp.broadcast_to(over, (HEAD, tokens)).T
    average_col = jnp.broadcast_to(average, (HEAD, tokens)).T
    over_all = jnp.concatenate([over_col] * GROUP, axis=0)
    average_all = jnp.concatenate([average_col] * GROUP, axis=0)
    for h in range(heads):
        cut = slice(h * HEAD, (h + 1) * HEAD)
        logits = logs[h]
        slope = sharpen * (1.0 - (logits / capping) ** 2)
        d_out = (slope * (-(expos[h] * over_all) * (logits - average_all))).astype(BF16)
        prob = probs[h]
        d_probs = lax.dot_general(
            kv[1, :, cut], d_out, (((1,), (1,)), ((), ())), preferred_element_type=F32
        )
        d_scores = (
            prob * (d_probs - jnp.sum(prob * d_probs, axis=0, keepdims=True))
        ).astype(BF16)
        d_keys = jnp.dot(d_scores, stacked(h), preferred_element_type=F32) * inverse
        d_values = jnp.dot(prob.astype(BF16), d_out, preferred_element_type=F32)
        dkv_out[0, :, cut] = d_keys.astype(BF16)
        dkv_out[1, :, cut] = d_values.astype(BF16)
    for copy in copies:
        copy.wait_send()


def attend(n_tensor, queries, kv):
    tokens = queries.shape[0]
    heads = kv.shape[2] // HEAD
    vmem = pl.BlockSpec(memory_space=pltpu.VMEM)
    dma = pltpu.SemaphoreType.DMA
    return pl.pallas_call(
        functools.partial(attend_kernel, n_tensor),
        out_shape=(
            jax.ShapeDtypeStruct(queries.shape, BF16),
            jax.ShapeDtypeStruct(kv.shape, BF16),
            jax.ShapeDtypeStruct((1, tokens), F32),
        ),
        in_specs=[vmem, vmem],
        out_specs=(vmem, vmem, vmem),
        scratch_shapes=[
            pltpu.VMEM((heads, tokens, GROUP * tokens), F32),
            pltpu.VMEM((heads, GROUP * tokens, HEAD), F32),
            pltpu.VMEM((heads, GROUP * tokens, HEAD), F32),
            pltpu.VMEM((n_tensor, 8, tokens), F32),
            dma((n_tensor,)), dma((n_tensor,)),
        ],
        compiler_params=pltpu.CompilerParams(
            collective_id=1, has_side_effects=True, vmem_limit_bytes=VMEM_BYTES
        ),
        name="attend",
    )(queries, kv)


def reduce_kernel(
    dims, n_tensor,
    dkv, rows_in, vectors, exps, ent, out,
    got, rows_v, vec_v, grads, held, held_t,
    local_sem, g_send, g_recv, t_send, t_recv, y_send, y_recv,
):
    outer, mid, inner = dims
    n_task = outer * mid * inner
    task, a, b, c = place(dims)
    y = lax.axis_index("tensor")
    tasks, mats, rows, cols = vectors.shape
    row_blocks, col_blocks = exps.shape[2:]
    near = [d for d in (2, 3, 1) if d < outer]
    order = [0] + near

    rows_copy = fetch(rows_in, rows_v, local_sem.at[0])
    vec_copy = fetch(vectors, vec_v, local_sem.at[1])

    def to(d, f, e):
        spot = index_of(dims, flip(a, d), turned(b, f, mid), turned(c, e, inner))
        return {"task": spot, "tensor": y}

    def source(d, f, e):
        return index_of(dims, flip(a, d), turned(b, -f, mid), turned(c, -e, inner))

    task_peers = [{"task": turned(task, s, n_task), "tensor": y} for s in range(1, n_task)]
    tensor_peers = [{"task": task, "tensor": turned(y, s, n_tensor)} for s in range(1, n_tensor)]
    meet(task_peers + tensor_peers)
    copies = {}

    def forward(m, held_at, hop):
        where = source(*held_at)
        slot = tuple(p + q for p, q in zip(held_at, hop))
        flat = ((m * outer + slot[0]) * mid + slot[1]) * inner + slot[2]
        copies[m, slot] = send(
            got.at[m, where] if any(held_at) else dkv.at[m],
            got.at[m, where],
            g_send.at[flat], g_recv.at[flat], to(*hop),
        )

    def take(m, slot):
        if any(slot):
            copies[m, slot].wait_recv()
        d, f, e = slot
        if not e:
            if not f:
                for step in range(1, mid):
                    forward(m, slot, (0, step, 0))
            for step in range(1, inner):
                forward(m, slot, (0, 0, step))
        where = source(*slot)
        block = got[m, where] if any(slot) else dkv[m]
        term = lax.dot_general(
            rows_v[where], block, (((0,), (0,)), ((), ())), preferred_element_type=F32
        )
        if any(slot):
            grads[m] += term
        else:
            grads[m] = term

    for m in range(mats):
        for d in near:
            forward(m, (0, 0, 0), (d, 0, 0))
    high = rows // row_blocks
    wide = cols // col_blocks

    def contracted(m):
        def contract(i, carry):
            these = pl.ds(pl.multiple_of(i * high, 8), high)
            carry = list(carry)
            for j in range(col_blocks):
                across = slice(j * wide, (j + 1) * wide)
                grad = grads[m, these, across]
                for t in range(tasks):
                    term = grad * vec_v[t, m, these, across].astype(F32)
                    term = jnp.sum(term.reshape(high // 8, 8, wide), axis=0)
                    carry[t] = carry[t] + scale_of(exps, t, m, i, j) * term
            return tuple(carry)

        start = tuple(jnp.zeros((8, wide), F32) for _ in range(tasks))
        return lax.fori_loop(0, row_blocks, contract, start)

    rows_copy.wait()
    lines = []
    for step in range(mats * outer + 2):
        if step == outer + 2:
            vec_copy.wait()
        if step > outer and (step - 2) % outer == 0:
            lines.append(contracted((step - 2) // outer - 1))
        slots = []
        if step < mats * outer:
            slots.append((step, 0, 0))
        if 1 <= step <= mats * outer:
            slots += [(step - 1, f, 0) for f in range(1, mid)]
            slots += [(step - 1, 0, e) for e in range(1, inner)]
        if step >= 2:
            slots += [(step - 2, f, e) for f in range(1, mid) for e in range(1, inner)]
        for at_step, f, e in slots:
            take(at_step // outer, (order[at_step % outer], f, e))
    while len(lines) < mats:
        if not lines:
            vec_copy.wait()
        lines.append(contracted(len(lines)))
    parts = [
        jnp.sum(lines[m][t], axis=0, keepdims=True) for t in range(tasks) for m in range(mats)
    ]
    entropy = jnp.broadcast_to(jnp.sum(ent[...]) / (n_tensor * wide), (1, wide))
    pad = -(len(parts) + 1) % 8
    stack = jnp.concatenate(parts + [entropy, jnp.zeros((pad, wide), F32)], axis=0)
    column = jnp.sum(stack, axis=1, keepdims=True)
    shape = (stack.shape[0], held.shape[2])
    along = lax.broadcasted_iota(jnp.int32, shape, 0) == lax.broadcasted_iota(jnp.int32, shape, 1)
    line = jnp.sum(jnp.where(along, column, 0.0), axis=0, keepdims=True)
    held[task] = jnp.broadcast_to(line, held.shape[1:])
    last = [
        send(held.at[task], held.at[task], t_send.at[s], t_recv.at[s], peer)
        for s, peer in enumerate(task_peers)
    ]
    for copy in last:
        copy.wait_recv()
    total = held[0]
    for k in range(1, n_task):
        total = total + held[k]
    held_t[y] = total
    more = [
        send(held_t.at[y], held_t.at[y], y_send.at[s], y_recv.at[s], peer)
        for s, peer in enumerate(tensor_peers)
    ]
    for copy in more:
        copy.wait_recv()
    total = held_t[0]
    for k in range(1, n_tensor):
        total = total + held_t[k]
    out[...] = total
    for copy in list(copies.values()) + last + more:
        copy.wait_send()


def reduce(dims, n_tensor, dkv, rows_in, vectors, exps, ent):
    n_task, tokens, rows = rows_in.shape
    tasks, mats, _, cols = vectors.shape
    vmem = pl.BlockSpec(memory_space=pltpu.VMEM)
    hbm = pl.BlockSpec(memory_space=pl.ANY)
    dma = pltpu.SemaphoreType.DMA
    return pl.pallas_call(
        functools.partial(reduce_kernel, dims, n_tensor),
        out_shape=jax.ShapeDtypeStruct((8, 128), F32),
        in_specs=[vmem, hbm, hbm, pl.BlockSpec(memory_space=pltpu.SMEM), vmem],
        out_specs=vmem,
        scratch_shapes=[
            pltpu.VMEM((mats, n_task, tokens, cols), BF16),
            pltpu.VMEM((n_task, tokens, rows), BF16),
            pltpu.VMEM(vectors.shape, BF16),
            pltpu.VMEM((mats, rows, cols), F32),
            pltpu.VMEM((n_task, 8, 128), F32),
            pltpu.VMEM((n_tensor, 8, 128), F32),
            dma((2,)),
            dma((mats * n_task,)), dma((mats * n_task,)),
            dma((n_task,)), dma((n_task,)),
            dma((n_tensor,)), dma((n_tensor,)),
        ],
        compiler_params=pltpu.CompilerParams(
            collective_id=2, has_side_effects=True, vmem_limit_bytes=VMEM_BYTES
        ),
        name="reduce",
    )(dkv, rows_in, vectors, exps, ent)


def local(inputs, queries, task_vectors, base_weights, scale_exps, coefs):
    n_task = lax.axis_size("task")
    n_tensor = lax.axis_size("tensor")
    dims = factors(n_task)
    tasks, mats = coefs.shape
    kv, rows_in = project(
        dims, n_tensor, inputs, task_vectors, base_weights, scale_exps, coefs
    )
    attended, dkv, ent = attend(n_tensor, queries, kv)
    sums = reduce(dims, n_tensor, dkv, rows_in, task_vectors, scale_exps, ent)
    coef_grad = sums[0, : tasks * mats].reshape(tasks, mats)
    mean_entropy = sums[0, tasks * mats] / (inputs.shape[0] * n_task)
    return (attended, mean_entropy, coef_grad)


def solution(mesh):
    return jax.shard_map(
        local,
        mesh=mesh,
        in_specs=(
            P("task", None),
            P("task", "tensor"),
            P(None, None, "task", "tensor"),
            P(None, "task", "tensor"),
            P(None, None, "task", "tensor"),
            P(),
        ),
        out_specs=(P("task", "tensor"), P(), P()),
        check_vma=False,
    )
```

```python
import functools
import math

import jax
import jax.numpy as jnp
from jax import lax
from jax.experimental import pallas as pl
from jax.experimental.pallas import tpu as pltpu
from jax.sharding import PartitionSpec as P

HEAD = 128
GROUP = 4

sharpen = 4.0
capping = 8.0
masked_value = -1e30

MESH = pl.DeviceIdType.MESH
VMEM_BYTES = 60 * 1024 * 1024
F32 = jnp.float32
BF16 = jnp.bfloat16


def factors(n_task):
    outer = math.gcd(n_task, 4)
    mid = math.gcd(n_task // outer, 2)
    return outer, mid, n_task // (outer * mid)


def place(dims):
    _, mid, inner = dims
    task = lax.axis_index("task")
    rest = lax.rem(task, mid * inner)
    return task, task // (mid * inner), rest // inner, lax.rem(rest, inner)


def turned(value, step, size):
    return lax.rem(value + (step + size), size)


def flip(value, step):
    bit = 1
    for_value = value
    while bit <= step:
        if step & bit:
            for_value = for_value + bit - 2 * bit * lax.rem(value // bit, 2)
        bit *= 2
    return for_value


def scale_of(exps, t, m, i, j):
    return lax.shift_left(jnp.int32(1), exps[t, m, i, j] + 3).astype(F32) * 0.125


def index_of(dims, a, b, c):
    _, mid, inner = dims
    return (a * mid + b) * inner + c


def meet(peers):
    sem = pltpu.get_barrier_semaphore()
    for peer in peers:
        pl.semaphore_signal(sem, inc=1, device_id=peer, device_id_type=MESH)
    pl.semaphore_wait(sem, len(peers))


def send(src, dst, send_sem, recv_sem, peer):
    copy = pltpu.make_async_remote_copy(
        src_ref=src,
        dst_ref=dst,
        send_sem=send_sem,
        recv_sem=recv_sem,
        device_id=peer,
        device_id_type=MESH,
    )
    copy.start()
    return copy


def fetch(src, dst, sem):
    copy = pltpu.make_async_copy(src, dst, sem)
    copy.start()
    return copy


def project_stage(
    dims, n_tensor, pieces,
    inputs, vectors, base, exps, coefs, greet,
    kv_out, rows_out,
    xin, mg, vec_v, base_v, acc, hold, pout, pin,
    local_sem, keep_sem, x_send, x_recv, y_send, y_recv, g_send, g_recv, r_send, r_recv, p_send, p_recv,
):
    outer, mid, inner = dims
    group = mid * inner
    task, a, b, c = place(dims)
    y = lax.axis_index("tensor")
    mine = b * inner + c
    tasks, mats, rows, cols = vectors.shape
    row_blocks, col_blocks = exps.shape[2:]
    tokens = inputs.shape[0]
    piece = tokens // pieces
    span = group * rows
    part = span // n_tensor
    turns = list(range(outer - 1, 0, -1))

    def at(a_, b_, c_):
        return {"task": index_of(dims, a_, b_, c_), "tensor": y}

    def tensor_peer(step):
        return {"task": task, "tensor": turned(y, step, n_tensor)}

    def group_peer(f, e):
        return at(a, turned(b, f, mid), turned(c, e, inner))

    def some(k):
        return slice(k * piece, (k + 1) * piece)

    base_copy = fetch(base, base_v, local_sem.at[0])
    vec_copies = [
        fetch(vectors.at[:, m], vec_v.at[:, m], local_sem.at[2 + m]) for m in range(mats)
    ]
    own_copy = fetch(
        inputs.at[:, pl.ds(pl.multiple_of(a * span, 128), span)], xin.at[a], local_sem.at[1]
    )
    greet()
    sent = []
    x_copies = {}
    own_cols = pl.ds(pl.multiple_of(y * part, 128), part)
    for k in range(pieces):
        for d in turns:
            to = flip(a, d)
            slot = d * pieces + k
            x_copies[k, d] = send(
                inputs.at[some(k), pl.ds(pl.multiple_of(to * span + y * part, 128), part)],
                xin.at[a, some(k), own_cols],
                x_send.at[slot], x_recv.at[slot], at(to, b, c),
            )
            sent.append(x_copies[k, d])
    high = rows // row_blocks
    wide = cols // col_blocks
    base_copy.wait()
    g_copies = {}

    def share(m, f, e, hop):
        came = turned(b, -(f - hop[0]), mid) * inner + turned(c, -(e - hop[1]), inner)
        slot = (m * mid + f) * inner + e
        g_copies[m, f, e] = send(
            mg.at[came, m], mg.at[came, m], g_send.at[slot], g_recv.at[slot], group_peer(*hop)
        )
        sent.append(g_copies[m, f, e])

    for m in range(mats):
        vec_copies[m].wait()

        def merge(i, carry):
            these = pl.ds(pl.multiple_of(i * high, 8), high)
            for j in range(col_blocks):
                across = slice(j * wide, (j + 1) * wide)
                total = base_v[m, these, across].astype(F32)
                for t in range(tasks):
                    scale = coefs[t, m] * scale_of(exps, t, m, i, j)
                    total += scale * vec_v[t, m, these, across].astype(F32)
                mg[mine, m, these, across] = total.astype(BF16)
            return carry

        lax.fori_loop(0, row_blocks, merge, 0)
        for f in range(1, mid):
            share(m, f, 0, (f, 0))
        for e in range(1, inner):
            share(m, 0, e, (0, e))

    r_copies = []
    keeps = []

    def spread(k, d):
        a_from = flip(a, d)
        owner = a_from * group + mine
        for f in range(mid):
            for e in range(inner):
                if not (f or e):
                    continue
                to = turned(b, f, mid) * inner + turned(c, e, inner)
                slot = ((k * outer + d) * mid + f) * inner + e
                r_copies.append(
                    send(
                        xin.at[a_from, some(k), pl.ds(pl.multiple_of(to * rows, 128), rows)],
                        rows_out.at[owner, some(k)],
                        r_send.at[slot], r_recv.at[slot], group_peer(f, e),
                    )
                )
        keeps.append(
            fetch(
                xin.at[a_from, some(k), pl.ds(pl.multiple_of(mine * rows, 128), rows)],
                rows_out.at[owner, some(k)],
                keep_sem.at[k * outer + d],
            )
        )

    y_copies = {}

    def pass_on(k):
        for d in turns:
            x_copies[k, d].wait_recv()
            block = xin.at[flip(a, d), some(k), own_cols]
            for s in range(1, n_tensor):
                slot = (k * outer + d) * n_tensor + s
                y_copies[k, d, s] = send(
                    block, block, y_send.at[slot], y_recv.at[slot], tensor_peer(s)
                )
                sent.append(y_copies[k, d, s])

    def share_on(m):
        for f in range(1, mid):
            g_copies[m, f, 0].wait_recv()
            for e in range(1, inner):
                share(m, f, e, (0, e))

    def own_part(m):
        for f in range(mid):
            for e in range(1, inner):
                g_copies[m, f, e].wait_recv()
        total = None
        for g in range(group):
            term = jnp.dot(
                xin[a, :, g * rows:(g + 1) * rows], mg[g, m], preferred_element_type=F32
            )
            total = term if total is None else total + term
        acc[m] = total

    p_copies = {}

    def give(k, m, d, to):
        slot = (d * pieces + k) * mats + m
        p_copies[k, m, d] = send(
            pout.at[d, m, some(k)], pin.at[d, m, some(k)],
            p_send.at[slot], p_recv.at[slot], at(flip(a, to), b, c),
        )
        sent.append(p_copies[k, m, d])

    def parts(k, m):
        if m == 0:
            for d in turns:
                for s in range(1, n_tensor):
                    y_copies[k, d, s].wait_recv()
        if not turns:
            return
        total = None
        for g in range(group):
            left = jnp.concatenate(
                [xin[flip(a, d), some(k), g * rows:(g + 1) * rows] for d in turns], axis=0
            )
            term = jnp.dot(left, mg[g, m], preferred_element_type=F32)
            total = term if total is None else total + term
        for n, d in enumerate(turns):
            mine_part = total[n * piece:(n + 1) * piece]
            if d == 2:
                hold[m, some(k)] = mine_part
            else:
                pout[d, m, some(k)] = mine_part.astype(BF16)
                give(k, m, d, 1)

    def combine(k, m):
        if 2 not in turns:
            return
        p_copies[k, m, 3].wait_recv()
        pout[2, m, some(k)] = (hold[m, some(k)] + pin[3, m, some(k)].astype(F32)).astype(BF16)
        give(k, m, 2, 2)

    last = pieces - 1
    pass_on(0)
    own_copy.wait()
    for k in range(pieces):
        spread(k, 0)
    share_on(0)
    for k in range(1, last):
        pass_on(k)
    own_part(0)
    for k in range(last):
        parts(k, 0)
        if k:
            combine(k - 1, 0)
        for d in turns:
            spread(k, d)
    share_on(1)
    if last:
        pass_on(last)
        combine(last - 1, 0)
    parts(last, 0)
    own_part(1)
    parts(0, 1)
    combine(last, 0)
    for k in range(1, pieces):
        parts(k, 1)
        combine(k - 1, 1)
    combine(last, 1)
    for d in turns:
        spread(last, d)
    for m in range(mats):
        for k in range(pieces):
            total = acc[m, some(k)]
            for d in turns:
                if d < 3:
                    p_copies[k, m, d].wait_recv()
                    total = total + pin[d, m, some(k)].astype(F32)
            kv_out[m, some(k)] = total.astype(BF16)
    return sent + r_copies, r_copies, keeps


def attend_stage(
    n_tensor, queries, kv, att_out, dkv_out, probs, logs, expos, sums, s_send, s_recv
):
    task = lax.axis_index("task")
    y = lax.axis_index("tensor")
    tokens = queries.shape[0]
    heads = kv.shape[2] // HEAD
    inverse = HEAD ** (-0.5)
    peers = [{"task": task, "tensor": turned(y, s, n_tensor)} for s in range(1, n_tensor)]
    key_at = lax.broadcasted_iota(jnp.int32, (tokens, GROUP * tokens), 0)
    query_at = lax.rem(lax.broadcasted_iota(jnp.int32, (tokens, GROUP * tokens), 1), tokens)
    causal = key_at <= query_at

    def stacked(h):
        return jnp.concatenate(
            [queries[:, (h * GROUP + r) * HEAD:(h * GROUP + r + 1) * HEAD] for r in range(GROUP)],
            axis=0,
        )

    total = jnp.zeros((tokens, HEAD), F32)
    moment = jnp.zeros((tokens, HEAD), F32)
    for h in range(heads):
        cut = slice(h * HEAD, (h + 1) * HEAD)
        scores = lax.dot_general(
            kv[0, :, cut], stacked(h), (((1,), (1,)), ((), ())), preferred_element_type=F32
        ) * inverse
        scores = jnp.where(causal, scores, masked_value)
        weight = jnp.exp(scores - jnp.max(scores, axis=0, keepdims=True))
        prob = weight * (1.0 / jnp.sum(weight, axis=0, keepdims=True))
        probs[h] = prob
        att = lax.dot_general(
            prob.astype(BF16), kv[1, :, cut], (((0,), (0,)), ((), ())), preferred_element_type=F32
        ).astype(BF16)
        logits = capping * jnp.tanh(sharpen * att.astype(F32) / capping)
        expo = jnp.exp(logits)
        logs[h] = logits
        expos[h] = expo
        scaled = expo * logits
        for r in range(GROUP):
            here = slice(r * tokens, (r + 1) * tokens)
            att_out[:, (h * GROUP + r) * HEAD:(h * GROUP + r + 1) * HEAD] = att[here]
            total += expo[here]
            moment += scaled[here]
    sums[y] = jnp.concatenate(
        [
            jnp.sum(total.T, axis=0, keepdims=True),
            jnp.sum(moment.T, axis=0, keepdims=True),
            jnp.zeros((6, tokens), F32),
        ],
        axis=0,
    )
    copies = [
        send(sums.at[y], sums.at[y], s_send.at[s], s_recv.at[s], peer)
        for s, peer in enumerate(peers)
    ]
    for copy in copies:
        copy.wait_recv()
    whole = sums[0]
    for s in range(1, n_tensor):
        whole = whole + sums[s]
    over = 1.0 / whole[0:1]
    average = whole[1:2] * over
    entropy = jnp.sum(jnp.log(whole[0:1]) - average)
    over_col = jnp.broadcast_to(over, (HEAD, tokens)).T
    average_col = jnp.broadcast_to(average, (HEAD, tokens)).T
    over_all = jnp.concatenate([over_col] * GROUP, axis=0)
    average_all = jnp.concatenate([average_col] * GROUP, axis=0)
    for h in range(heads):
        cut = slice(h * HEAD, (h + 1) * HEAD)
        logits = logs[h]
        slope = sharpen * (1.0 - (logits / capping) ** 2)
        d_out = (slope * (-(expos[h] * over_all) * (logits - average_all))).astype(BF16)
        prob = probs[h]
        d_probs = lax.dot_general(
            kv[1, :, cut], d_out, (((1,), (1,)), ((), ())), preferred_element_type=F32
        )
        d_scores = (
            prob * (d_probs - jnp.sum(prob * d_probs, axis=0, keepdims=True))
        ).astype(BF16)
        d_keys = jnp.dot(d_scores, stacked(h), preferred_element_type=F32) * inverse
        d_values = jnp.dot(prob.astype(BF16), d_out, preferred_element_type=F32)
        dkv_out[0, :, cut] = d_keys.astype(BF16)
        dkv_out[1, :, cut] = d_values.astype(BF16)
    return copies, entropy


def reduce_stage(
    dims, n_tensor, task_peers, tensor_peers, rows_ready, entropy,
    dkv, exps, grad_out, mean_out,
    got, rows_v, vec_v, grads, held, held_t,
    g_send, g_recv, t_send, t_recv, y_send, y_recv,
):
    outer, mid, inner = dims
    n_task = outer * mid * inner
    task, a, b, c = place(dims)
    y = lax.axis_index("tensor")
    tasks, mats, rows, cols = vec_v.shape
    row_blocks, col_blocks = exps.shape[2:]
    near = [d for d in (2, 1, 3) if d < outer]
    order = [0] + near

    def to(d, f, e):
        spot = index_of(dims, flip(a, d), turned(b, f, mid), turned(c, e, inner))
        return {"task": spot, "tensor": y}

    def source(d, f, e):
        return index_of(dims, flip(a, d), turned(b, -f, mid), turned(c, -e, inner))

    copies = {}

    def forward(m, held_at, hop):
        where = source(*held_at)
        slot = tuple(p + q for p, q in zip(held_at, hop))
        flat = ((m * outer + slot[0]) * mid + slot[1]) * inner + slot[2]
        copies[m, slot] = send(
            got.at[m, where] if any(held_at) else dkv.at[m],
            got.at[m, where],
            g_send.at[flat], g_recv.at[flat], to(*hop),
        )

    def take(m, slot):
        if any(slot):
            copies[m, slot].wait_recv()
        d, f, e = slot
        if not e:
            if d and not f:
                for step in range(1, mid):
                    forward(m, slot, (0, step, 0))
            for step in range(1, inner):
                forward(m, slot, (0, 0, step))
        where = source(*slot)
        block = got[m, where] if any(slot) else dkv[m]
        term = lax.dot_general(
            rows_v[where], block, (((0,), (0,)), ((), ())), preferred_element_type=F32
        )
        if any(slot):
            grads[m] += term
        else:
            grads[m] = term

    for m in range(mats):
        for d in near:
            forward(m, (0, 0, 0), (d, 0, 0))
        for step in range(1, mid):
            forward(m, (0, 0, 0), (0, step, 0))
    high = rows // row_blocks
    wide = cols // col_blocks

    def contracted(m):
        def contract(i, carry):
            these = pl.ds(pl.multiple_of(i * high, 8), high)
            carry = list(carry)
            for j in range(col_blocks):
                across = slice(j * wide, (j + 1) * wide)
                grad = grads[m, these, across]
                for t in range(tasks):
                    term = grad * vec_v[t, m, these, across].astype(F32)
                    term = jnp.sum(term.reshape(high // 8, 8, wide), axis=0)
                    carry[t] = carry[t] + scale_of(exps, t, m, i, j) * term
            return tuple(carry)

        start = tuple(jnp.zeros((8, wide), F32) for _ in range(tasks))
        return lax.fori_loop(0, row_blocks, contract, start)

    rows_ready()
    lines = []
    for step in range(mats * outer + 2):
        if step > outer and (step - 2) % outer == 0:
            lines.append(contracted((step - 2) // outer - 1))
        slots = []
        if step < mats * outer:
            slots.append((step, 0, 0))
        if 1 <= step <= mats * outer:
            slots += [(step - 1, f, 0) for f in range(1, mid)]
            slots += [(step - 1, 0, e) for e in range(1, inner)]
        if step >= 2:
            slots += [(step - 2, f, e) for f in range(1, mid) for e in range(1, inner)]
        for at_step, f, e in slots:
            take(at_step // outer, (order[at_step % outer], f, e))
    while len(lines) < mats:
        lines.append(contracted(len(lines)))
    parts = [
        jnp.sum(lines[m][t], axis=0, keepdims=True) for t in range(tasks) for m in range(mats)
    ]
    entropy = jnp.broadcast_to(entropy / (n_tensor * wide), (1, wide))
    pad = -(len(parts) + 1) % 8
    stack = jnp.concatenate(parts + [entropy, jnp.zeros((pad, wide), F32)], axis=0)
    column = jnp.sum(stack, axis=1, keepdims=True)
    shape = (stack.shape[0], held.shape[2])
    along = lax.broadcasted_iota(jnp.int32, shape, 0) == lax.broadcasted_iota(jnp.int32, shape, 1)
    line = jnp.sum(jnp.where(along, column, 0.0), axis=0, keepdims=True)
    held[task] = jnp.broadcast_to(line, held.shape[1:])
    last = [
        send(held.at[task], held.at[task], t_send.at[s], t_recv.at[s], peer)
        for s, peer in enumerate(task_peers)
    ]
    for copy in last:
        copy.wait_recv()
    total = held[0]
    for k in range(1, n_task):
        total = total + held[k]
    held_t[y] = total
    more = [
        send(held_t.at[y], held_t.at[y], y_send.at[s], y_recv.at[s], peer)
        for s, peer in enumerate(tensor_peers)
    ]
    for copy in more:
        copy.wait_recv()
    total = held_t[0]
    for k in range(1, n_tensor):
        total = total + held_t[k]
    tokens = rows_v.shape[1]
    mean_out[...] = total[0:1, tasks * mats:tasks * mats + 1] * (1.0 / (tokens * n_task))
    line = jnp.broadcast_to(total[0:1], (tasks, total.shape[1]))
    which = lax.broadcasted_iota(jnp.int32, line.shape, 1) - mats * lax.broadcasted_iota(
        jnp.int32, line.shape, 0
    )
    at_mat = lax.broadcasted_iota(jnp.int32, (tasks, mats), 1)
    result = jnp.zeros((tasks, mats), F32)
    for m in range(mats):
        column = jnp.sum(jnp.where(which == m, line, 0.0), axis=1, keepdims=True)
        result = jnp.where(at_mat == m, column, result)
    grad_out[...] = result
    return list(copies.values()) + last + more


def whole_kernel(
    dims, n_tensor, pieces,
    inputs, queries, vectors, base, exps, coefs,
    att_hbm, mean_out, grad_out,
    xin, mg, vec_v, base_v, acc, hold, pout, pin, kv, rows_v, att, dkv, probs, logs, expos, sums,
    got, grads, held, held_t, out_sem,
    local_sem, keep_sem, x_send, x_recv, y_send, y_recv, g_send, g_recv, r_send, r_recv, p_send, p_recv,
    s_send, s_recv, d_send, d_recv, t_send, t_recv, z_send, z_recv,
):
    n_task = dims[0] * dims[1] * dims[2]
    task = lax.axis_index("task")
    y = lax.axis_index("tensor")
    task_peers = [{"task": turned(task, s, n_task), "tensor": y} for s in range(1, n_task)]
    tensor_peers = [{"task": task, "tensor": turned(y, s, n_tensor)} for s in range(1, n_tensor)]

    def greet():
        meet(task_peers + tensor_peers)

    sent, r_copies, keeps = project_stage(
        dims, n_tensor, pieces, inputs, vectors, base, exps, coefs, greet, kv, rows_v,
        xin, mg, vec_v, base_v, acc, hold, pout, pin,
        local_sem, keep_sem, x_send, x_recv, y_send, y_recv, g_send, g_recv, r_send, r_recv, p_send, p_recv,
    )
    exchanged, entropy = attend_stage(
        n_tensor, queries, kv, att, dkv, probs, logs, expos, sums, s_send, s_recv
    )
    att_copy = fetch(att, att_hbm, out_sem)

    def rows_ready():
        for copy in keeps:
            copy.wait()
        for copy in r_copies:
            copy.wait_recv()

    more = reduce_stage(
        dims, n_tensor, task_peers, tensor_peers, rows_ready, entropy, dkv, exps, grad_out, mean_out,
        got, rows_v, vec_v, grads, held, held_t,
        d_send, d_recv, t_send, t_recv, z_send, z_recv,
    )
    att_copy.wait()
    for copy in sent + exchanged + more:
        copy.wait_send()


def local(inputs, queries, task_vectors, base_weights, scale_exps, coefs):
    n_task = lax.axis_size("task")
    n_tensor = lax.axis_size("tensor")
    dims = factors(n_task)
    outer, mid, inner = dims
    group = mid * inner
    tokens = inputs.shape[0]
    tasks, mats, rows, cols = task_vectors.shape
    heads = cols // HEAD
    pieces = math.gcd(tokens // 16, 3)
    hbm = pl.BlockSpec(memory_space=pl.ANY)
    vmem = pl.BlockSpec(memory_space=pltpu.VMEM)
    smem = pl.BlockSpec(memory_space=pltpu.SMEM)
    dma = pltpu.SemaphoreType.DMA

    def pair(count):
        return [dma((count,)), dma((count,))]

    attended, mean_entropy, coef_grad = pl.pallas_call(
        functools.partial(whole_kernel, dims, n_tensor, pieces),
        out_shape=(
            jax.ShapeDtypeStruct(queries.shape, BF16),
            jax.ShapeDtypeStruct((1, 1), F32),
            jax.ShapeDtypeStruct((tasks, mats), F32),
        ),
        in_specs=[hbm, vmem, hbm, hbm, smem, smem],
        out_specs=(hbm, vmem, vmem),
        scratch_shapes=[
            pltpu.VMEM((outer, tokens, group * rows), BF16),
            pltpu.VMEM((group, mats, rows, cols), BF16),
            pltpu.VMEM(task_vectors.shape, BF16),
            pltpu.VMEM(base_weights.shape, BF16),
            pltpu.VMEM((mats, tokens, cols), F32),
            pltpu.VMEM((mats, tokens, cols), F32),
            pltpu.VMEM((outer, mats, tokens, cols), BF16),
            pltpu.VMEM((outer, mats, tokens, cols), BF16),
            pltpu.VMEM((mats, tokens, cols), BF16),
            pltpu.VMEM((n_task, tokens, rows), BF16),
            pltpu.VMEM(queries.shape, BF16),
            pltpu.VMEM((mats, tokens, cols), BF16),
            pltpu.VMEM((heads, tokens, GROUP * tokens), F32),
            pltpu.VMEM((heads, GROUP * tokens, HEAD), F32),
            pltpu.VMEM((heads, GROUP * tokens, HEAD), F32),
            pltpu.VMEM((n_tensor, 8, tokens), F32),
            pltpu.VMEM((mats, n_task, tokens, cols), BF16),
            pltpu.VMEM((mats, rows, cols), F32),
            pltpu.VMEM((n_task, 8, 128), F32),
            pltpu.VMEM((n_tensor, 8, 128), F32),
            dma,
            dma((2 + mats,)), dma((pieces * outer,)),
            *pair(outer * pieces),
            *pair(pieces * outer * n_tensor),
            *pair(mats * group),
            *pair(pieces * n_task),
            *pair(outer * pieces * mats),
            *pair(n_tensor),
            *pair(mats * n_task),
            *pair(n_task),
            *pair(n_tensor),
        ],
        compiler_params=pltpu.CompilerParams(
            collective_id=0, has_side_effects=True, vmem_limit_bytes=VMEM_BYTES
        ),
        name="whole",
    )(inputs, queries, task_vectors, base_weights, scale_exps, coefs)
    return (attended, mean_entropy[0, 0], coef_grad)


def solution(mesh):
    return jax.shard_map(
        local,
        mesh=mesh,
        in_specs=(
            P("task", None),
            P("task", "tensor"),
            P(None, None, "task", "tensor"),
            P(None, "task", "tensor"),
            P(None, None, "task", "tensor"),
            P(),
        ),
        out_specs=(P("task", "tensor"), P(), P()),
        check_vma=False,
    )
```

```python
import functools
import math

import jax
import jax.numpy as jnp
from jax import lax
from jax.experimental import pallas as pl
from jax.experimental.pallas import tpu as pltpu
from jax.sharding import PartitionSpec as P

HEAD = 128
GROUP = 4

sharpen = 4.0
capping = 8.0
masked_value = -1e30

MESH = pl.DeviceIdType.MESH
VMEM_BYTES = 60 * 1024 * 1024
F32 = jnp.float32
BF16 = jnp.bfloat16


def factors(n_task):
    outer = math.gcd(n_task, 4)
    mid = math.gcd(n_task // outer, 2)
    return outer, mid, n_task // (outer * mid)


def place(dims):
    _, mid, inner = dims
    task = lax.axis_index("task")
    rest = lax.rem(task, mid * inner)
    return task, task // (mid * inner), rest // inner, lax.rem(rest, inner)


def turned(value, step, size):
    return lax.rem(value + (step + size), size)


def flip(value, step):
    bit = 1
    for_value = value
    while bit <= step:
        if step & bit:
            for_value = for_value + bit - 2 * bit * lax.rem(value // bit, 2)
        bit *= 2
    return for_value


def scale_of(exps, t, m, i, j):
    return lax.shift_left(jnp.int32(1), exps[m, i, j, t] + 3).astype(F32) * 0.125


def index_of(dims, a, b, c):
    _, mid, inner = dims
    return (a * mid + b) * inner + c


def meet(peers):
    sem = pltpu.get_barrier_semaphore()
    for peer in peers:
        pl.semaphore_signal(sem, inc=1, device_id=peer, device_id_type=MESH)
    pl.semaphore_wait(sem, len(peers))


def send(src, dst, send_sem, recv_sem, peer):
    copy = pltpu.make_async_remote_copy(
        src_ref=src,
        dst_ref=dst,
        send_sem=send_sem,
        recv_sem=recv_sem,
        device_id=peer,
        device_id_type=MESH,
    )
    copy.start()
    return copy


def fetch(src, dst, sem):
    copy = pltpu.make_async_copy(src, dst, sem)
    copy.start()
    return copy


def project_stage(
    dims, n_tensor, pieces,
    inputs, vectors, base, exps, coefs, greet,
    kv_out, rows_out,
    xin, mg, vec_v, base_v, acc, hold, pout, pin,
    local_sem, keep_sem, x_send, x_recv, y_send, y_recv, g_send, g_recv, r_send, r_recv, p_send, p_recv,
):
    outer, mid, inner = dims
    group = mid * inner
    task, a, b, c = place(dims)
    y = lax.axis_index("tensor")
    mine = b * inner + c
    tasks, mats, rows, cols = vectors.shape
    row_blocks, col_blocks = exps.shape[1:3]
    tokens = inputs.shape[0]
    piece = tokens // pieces
    span = group * rows
    part = span // n_tensor
    turns = list(range(outer - 1, 0, -1))

    def at(a_, b_, c_):
        return {"task": index_of(dims, a_, b_, c_), "tensor": y}

    def tensor_peer(step):
        return {"task": task, "tensor": turned(y, step, n_tensor)}

    def group_peer(f, e):
        return at(a, turned(b, f, mid), turned(c, e, inner))

    def some(k):
        return slice(k * piece, (k + 1) * piece)

    base_copy = fetch(base, base_v, local_sem.at[0])
    vec_copies = [
        fetch(vectors.at[:, m], vec_v.at[:, m], local_sem.at[2 + m]) for m in range(mats)
    ]
    own_copy = fetch(
        inputs.at[:, pl.ds(pl.multiple_of(a * span, 128), span)], xin.at[a], local_sem.at[1]
    )
    greet()
    sent = []
    x_copies = {}
    own_cols = pl.ds(pl.multiple_of(y * part, 128), part)
    for k in range(pieces):
        for d in turns:
            to = flip(a, d)
            slot = d * pieces + k
            x_copies[k, d] = send(
                inputs.at[some(k), pl.ds(pl.multiple_of(to * span + y * part, 128), part)],
                xin.at[a, some(k), own_cols],
                x_send.at[slot], x_recv.at[slot], at(to, b, c),
            )
            sent.append(x_copies[k, d])
    high = rows // row_blocks
    wide = cols // col_blocks
    base_copy.wait()
    g_copies = {}

    def share(m, f, e, hop):
        came = turned(b, -(f - hop[0]), mid) * inner + turned(c, -(e - hop[1]), inner)
        slot = (m * mid + f) * inner + e
        g_copies[m, f, e] = send(
            mg.at[came, m], mg.at[came, m], g_send.at[slot], g_recv.at[slot], group_peer(*hop)
        )
        sent.append(g_copies[m, f, e])

    for m in range(mats):
        vec_copies[m].wait()

        def merge(i, carry):
            these = pl.ds(pl.multiple_of(i * high, 8), high)
            for j in range(col_blocks):
                across = slice(j * wide, (j + 1) * wide)
                total = base_v[m, these, across].astype(F32)
                for t in range(tasks):
                    scale = coefs[m, t] * scale_of(exps, t, m, i, j)
                    total += scale * vec_v[t, m, these, across].astype(F32)
                mg[mine, m, these, across] = total.astype(BF16)
            return carry

        lax.fori_loop(0, row_blocks, merge, 0)
        for f in range(1, mid):
            share(m, f, 0, (f, 0))
        for e in range(1, inner):
            share(m, 0, e, (0, e))

    r_copies = []
    keeps = []

    def spread(k, d):
        a_from = flip(a, d)
        owner = a_from * group + mine
        for f in range(mid):
            for e in range(inner):
                if not (f or e):
                    continue
                to = turned(b, f, mid) * inner + turned(c, e, inner)
                slot = ((k * outer + d) * mid + f) * inner + e
                r_copies.append(
                    send(
                        xin.at[a_from, some(k), pl.ds(pl.multiple_of(to * rows, 128), rows)],
                        rows_out.at[owner, some(k)],
                        r_send.at[slot], r_recv.at[slot], group_peer(f, e),
                    )
                )
        keeps.append(
            fetch(
                xin.at[a_from, some(k), pl.ds(pl.multiple_of(mine * rows, 128), rows)],
                rows_out.at[owner, some(k)],
                keep_sem.at[k * outer + d],
            )
        )

    y_copies = {}

    def pass_on(k):
        for d in turns:
            x_copies[k, d].wait_recv()
            block = xin.at[flip(a, d), some(k), own_cols]
            for s in range(1, n_tensor):
                slot = (k * outer + d) * n_tensor + s
                y_copies[k, d, s] = send(
                    block, block, y_send.at[slot], y_recv.at[slot], tensor_peer(s)
                )
                sent.append(y_copies[k, d, s])

    def share_on(m):
        for f in range(1, mid):
            g_copies[m, f, 0].wait_recv()
            for e in range(1, inner):
                share(m, f, e, (0, e))

    def own_part(m):
        for f in range(mid):
            for e in range(1, inner):
                g_copies[m, f, e].wait_recv()
        total = None
        for g in range(group):
            term = jnp.dot(
                xin[a, :, g * rows:(g + 1) * rows], mg[g, m], preferred_element_type=F32
            )
            total = term if total is None else total + term
        acc[m] = total

    p_copies = {}

    def give(k, m, d, to):
        slot = (d * pieces + k) * mats + m
        p_copies[k, m, d] = send(
            pout.at[d, m, some(k)], pin.at[d, m, some(k)],
            p_send.at[slot], p_recv.at[slot], at(flip(a, to), b, c),
        )
        sent.append(p_copies[k, m, d])

    def parts(k, m):
        if m == 0:
            for d in turns:
                for s in range(1, n_tensor):
                    y_copies[k, d, s].wait_recv()
        if not turns:
            return
        total = None
        for g in range(group):
            left = jnp.concatenate(
                [xin[flip(a, d), some(k), g * rows:(g + 1) * rows] for d in turns], axis=0
            )
            term = jnp.dot(left, mg[g, m], preferred_element_type=F32)
            total = term if total is None else total + term
        for n, d in enumerate(turns):
            mine_part = total[n * piece:(n + 1) * piece]
            if d == 2:
                hold[m, some(k)] = mine_part
            else:
                pout[d, m, some(k)] = mine_part.astype(BF16)
                give(k, m, d, 1)

    def combine(k, m):
        if 2 not in turns:
            return
        p_copies[k, m, 3].wait_recv()
        pout[2, m, some(k)] = (hold[m, some(k)] + pin[3, m, some(k)].astype(F32)).astype(BF16)
        give(k, m, 2, 2)

    last = pieces - 1
    pass_on(0)
    own_copy.wait()
    for k in range(pieces):
        spread(k, 0)
    share_on(0)
    for k in range(1, last):
        pass_on(k)
    own_part(0)
    for k in range(last):
        parts(k, 0)
        if k:
            combine(k - 1, 0)
        for d in turns:
            spread(k, d)
    share_on(1)
    if last:
        pass_on(last)
        combine(last - 1, 0)
    parts(last, 0)
    own_part(1)
    parts(0, 1)
    combine(last, 0)
    for k in range(1, pieces):
        parts(k, 1)
        combine(k - 1, 1)
    combine(last, 1)
    for d in turns:
        spread(last, d)
    for m in range(mats):
        for k in range(pieces):
            total = acc[m, some(k)]
            for d in turns:
                if d < 3:
                    p_copies[k, m, d].wait_recv()
                    total = total + pin[d, m, some(k)].astype(F32)
            kv_out[m, some(k)] = total.astype(BF16)
    return sent + r_copies, r_copies, keeps


def attend_stage(
    n_tensor, queries, kv, att_out, dkv_out, probs, logs, expos, sums, s_send, s_recv
):
    task = lax.axis_index("task")
    y = lax.axis_index("tensor")
    tokens = queries.shape[0]
    heads = kv.shape[2] // HEAD
    inverse = HEAD ** (-0.5)
    peers = [{"task": task, "tensor": turned(y, s, n_tensor)} for s in range(1, n_tensor)]
    key_at = lax.broadcasted_iota(jnp.int32, (tokens, GROUP * tokens), 0)
    query_at = lax.rem(lax.broadcasted_iota(jnp.int32, (tokens, GROUP * tokens), 1), tokens)
    causal = key_at <= query_at

    def stacked(h):
        return jnp.concatenate(
            [queries[:, (h * GROUP + r) * HEAD:(h * GROUP + r + 1) * HEAD] for r in range(GROUP)],
            axis=0,
        )

    total = jnp.zeros((tokens, HEAD), F32)
    moment = jnp.zeros((tokens, HEAD), F32)
    for h in range(heads):
        cut = slice(h * HEAD, (h + 1) * HEAD)
        scores = lax.dot_general(
            kv[0, :, cut], stacked(h), (((1,), (1,)), ((), ())), preferred_element_type=F32
        ) * inverse
        scores = jnp.where(causal, scores, masked_value)
        weight = jnp.exp(scores - jnp.max(scores, axis=0, keepdims=True))
        prob = weight * (1.0 / jnp.sum(weight, axis=0, keepdims=True))
        probs[h] = prob
        att = lax.dot_general(
            prob.astype(BF16), kv[1, :, cut], (((0,), (0,)), ((), ())), preferred_element_type=F32
        ).astype(BF16)
        logits = capping * jnp.tanh(sharpen * att.astype(F32) / capping)
        expo = jnp.exp(logits)
        logs[h] = logits
        expos[h] = expo
        scaled = expo * logits
        for r in range(GROUP):
            here = slice(r * tokens, (r + 1) * tokens)
            att_out[:, (h * GROUP + r) * HEAD:(h * GROUP + r + 1) * HEAD] = att[here]
            total += expo[here]
            moment += scaled[here]
    sums[y] = jnp.concatenate(
        [
            jnp.sum(total.T, axis=0, keepdims=True),
            jnp.sum(moment.T, axis=0, keepdims=True),
            jnp.zeros((6, tokens), F32),
        ],
        axis=0,
    )
    copies = [
        send(sums.at[y], sums.at[y], s_send.at[s], s_recv.at[s], peer)
        for s, peer in enumerate(peers)
    ]
    for copy in copies:
        copy.wait_recv()
    whole = sums[0]
    for s in range(1, n_tensor):
        whole = whole + sums[s]
    over = 1.0 / whole[0:1]
    average = whole[1:2] * over
    entropy = jnp.sum(jnp.log(whole[0:1]) - average)
    over_col = jnp.broadcast_to(over, (HEAD, tokens)).T
    average_col = jnp.broadcast_to(average, (HEAD, tokens)).T
    over_all = jnp.concatenate([over_col] * GROUP, axis=0)
    average_all = jnp.concatenate([average_col] * GROUP, axis=0)
    for h in range(heads):
        cut = slice(h * HEAD, (h + 1) * HEAD)
        logits = logs[h]
        slope = sharpen * (1.0 - (logits / capping) ** 2)
        d_out = (slope * (-(expos[h] * over_all) * (logits - average_all))).astype(BF16)
        prob = probs[h]
        d_probs = lax.dot_general(
            kv[1, :, cut], d_out, (((1,), (1,)), ((), ())), preferred_element_type=F32
        )
        d_scores = (
            prob * (d_probs - jnp.sum(prob * d_probs, axis=0, keepdims=True))
        ).astype(BF16)
        d_keys = jnp.dot(d_scores, stacked(h), preferred_element_type=F32) * inverse
        d_values = jnp.dot(prob.astype(BF16), d_out, preferred_element_type=F32)
        dkv_out[0, :, cut] = d_keys.astype(BF16)
        dkv_out[1, :, cut] = d_values.astype(BF16)
    return copies, entropy


def reduce_stage(
    dims, n_tensor, task_peers, tensor_peers, rows_ready, entropy,
    dkv, exps, grad_out, mean_out,
    got, rows_v, vec_v, grads, held, held_t,
    g_send, g_recv, t_send, t_recv, y_send, y_recv,
):
    outer, mid, inner = dims
    n_task = outer * mid * inner
    task, a, b, c = place(dims)
    y = lax.axis_index("tensor")
    tasks, mats, rows, cols = vec_v.shape
    row_blocks, col_blocks = exps.shape[1:3]
    near = [d for d in (2, 1, 3) if d < outer]
    order = [0] + near

    def to(d, f, e):
        spot = index_of(dims, flip(a, d), turned(b, f, mid), turned(c, e, inner))
        return {"task": spot, "tensor": y}

    def source(d, f, e):
        return index_of(dims, flip(a, d), turned(b, -f, mid), turned(c, -e, inner))

    copies = {}

    def forward(m, held_at, hop):
        where = source(*held_at)
        slot = tuple(p + q for p, q in zip(held_at, hop))
        flat = ((m * outer + slot[0]) * mid + slot[1]) * inner + slot[2]
        copies[m, slot] = send(
            got.at[m, where] if any(held_at) else dkv.at[m],
            got.at[m, where],
            g_send.at[flat], g_recv.at[flat], to(*hop),
        )

    def take(m, slot):
        if any(slot):
            copies[m, slot].wait_recv()
        d, f, e = slot
        if not e:
            if d and not f:
                for step in range(1, mid):
                    forward(m, slot, (0, step, 0))
            for step in range(1, inner):
                forward(m, slot, (0, 0, step))
        where = source(*slot)
        block = got[m, where] if any(slot) else dkv[m]
        term = lax.dot_general(
            rows_v[where], block, (((0,), (0,)), ((), ())), preferred_element_type=F32
        )
        if any(slot):
            grads[m] += term
        else:
            grads[m] = term

    for m in range(mats):
        for d in near:
            forward(m, (0, 0, 0), (d, 0, 0))
        for step in range(1, mid):
            forward(m, (0, 0, 0), (0, step, 0))
    high = rows // row_blocks
    wide = cols // col_blocks

    def contracted(m):
        def contract(i, carry):
            these = pl.ds(pl.multiple_of(i * high, 8), high)
            carry = list(carry)
            for j in range(col_blocks):
                across = slice(j * wide, (j + 1) * wide)
                grad = grads[m, these, across]
                for t in range(tasks):
                    term = grad * vec_v[t, m, these, across].astype(F32)
                    term = jnp.sum(term.reshape(high // 8, 8, wide), axis=0)
                    carry[t] = carry[t] + scale_of(exps, t, m, i, j) * term
            return tuple(carry)

        start = tuple(jnp.zeros((8, wide), F32) for _ in range(tasks))
        return lax.fori_loop(0, row_blocks, contract, start)

    rows_ready()
    lines = []
    for step in range(mats * outer + 2):
        if step > outer and (step - 2) % outer == 0:
            lines.append(contracted((step - 2) // outer - 1))
        slots = []
        if step < mats * outer:
            slots.append((step, 0, 0))
        if 1 <= step <= mats * outer:
            slots += [(step - 1, f, 0) for f in range(1, mid)]
            slots += [(step - 1, 0, e) for e in range(1, inner)]
        if step >= 2:
            slots += [(step - 2, f, e) for f in range(1, mid) for e in range(1, inner)]
        for at_step, f, e in slots:
            take(at_step // outer, (order[at_step % outer], f, e))
    while len(lines) < mats:
        lines.append(contracted(len(lines)))
    parts = [
        jnp.sum(lines[m][t], axis=0, keepdims=True) for t in range(tasks) for m in range(mats)
    ]
    entropy = jnp.broadcast_to(entropy / (n_tensor * wide), (1, wide))
    pad = -(len(parts) + 1) % 8
    stack = jnp.concatenate(parts + [entropy, jnp.zeros((pad, wide), F32)], axis=0)
    column = jnp.sum(stack, axis=1, keepdims=True)
    shape = (stack.shape[0], held.shape[2])
    along = lax.broadcasted_iota(jnp.int32, shape, 0) == lax.broadcasted_iota(jnp.int32, shape, 1)
    line = jnp.sum(jnp.where(along, column, 0.0), axis=0, keepdims=True)
    held[task] = jnp.broadcast_to(line, held.shape[1:])
    last = [
        send(held.at[task], held.at[task], t_send.at[s], t_recv.at[s], peer)
        for s, peer in enumerate(task_peers)
    ]
    for copy in last:
        copy.wait_recv()
    total = held[0]
    for k in range(1, n_task):
        total = total + held[k]
    held_t[y] = total
    more = [
        send(held_t.at[y], held_t.at[y], y_send.at[s], y_recv.at[s], peer)
        for s, peer in enumerate(tensor_peers)
    ]
    for copy in more:
        copy.wait_recv()
    total = held_t[0]
    for k in range(1, n_tensor):
        total = total + held_t[k]
    tokens = rows_v.shape[1]
    mean_out[...] = total[0:1, tasks * mats:tasks * mats + 1] * (1.0 / (tokens * n_task))
    wide_line = jnp.broadcast_to(total[0:1], (tasks, total.shape[1]))
    spot = lax.broadcasted_iota(jnp.int32, wide_line.shape, 1)
    task_at = lax.broadcasted_iota(jnp.int32, wide_line.shape, 0)
    grid = (mats, total.shape[1])
    mat_at = lax.broadcasted_iota(jnp.int32, grid, 0)
    result = jnp.zeros(grid, F32)
    for m in range(mats):
        column = jnp.sum(jnp.where(spot == mats * task_at + m, wide_line, 0.0), axis=1, keepdims=True)
        row = jnp.sum(jnp.where(spot == task_at, column, 0.0), axis=0, keepdims=True)
        result = jnp.where(mat_at == m, row, result)
    grad_out[...] = result[:, :tasks]
    return list(copies.values()) + last + more


def whole_kernel(
    dims, n_tensor, pieces,
    inputs, queries, vectors, base, exps, coefs,
    att, mean_out, grad_out,
    xin, mg, vec_v, base_v, acc, hold, pout, pin, kv, rows_v, dkv, probs, logs, expos, sums,
    got, grads, held, held_t, smem_sem, exps_v, coefs_v,
    local_sem, keep_sem, x_send, x_recv, y_send, y_recv, g_send, g_recv, r_send, r_recv, p_send, p_recv,
    s_send, s_recv, d_send, d_recv, t_send, t_recv, z_send, z_recv,
):
    n_task = dims[0] * dims[1] * dims[2]
    task = lax.axis_index("task")
    y = lax.axis_index("tensor")
    task_peers = [{"task": turned(task, s, n_task), "tensor": y} for s in range(1, n_task)]
    tensor_peers = [{"task": task, "tensor": turned(y, s, n_tensor)} for s in range(1, n_tensor)]

    small = [fetch(exps, exps_v, smem_sem.at[0]), fetch(coefs, coefs_v, smem_sem.at[1])]

    def greet():
        meet(task_peers + tensor_peers)
        for copy in small:
            copy.wait()

    sent, r_copies, keeps = project_stage(
        dims, n_tensor, pieces, inputs, vectors, base, exps_v, coefs_v, greet, kv, rows_v,
        xin, mg, vec_v, base_v, acc, hold, pout, pin,
        local_sem, keep_sem, x_send, x_recv, y_send, y_recv, g_send, g_recv, r_send, r_recv, p_send, p_recv,
    )
    exchanged, entropy = attend_stage(
        n_tensor, queries, kv, att, dkv, probs, logs, expos, sums, s_send, s_recv
    )

    def rows_ready():
        for copy in keeps:
            copy.wait()
        for copy in r_copies:
            copy.wait_recv()

    more = reduce_stage(
        dims, n_tensor, task_peers, tensor_peers, rows_ready, entropy, dkv, exps_v, grad_out, mean_out,
        got, rows_v, vec_v, grads, held, held_t,
        d_send, d_recv, t_send, t_recv, z_send, z_recv,
    )
    for copy in sent + exchanged + more:
        copy.wait_send()


def local(inputs, queries, task_vectors, base_weights, scale_exps, coefs):
    n_task = lax.axis_size("task")
    n_tensor = lax.axis_size("tensor")
    dims = factors(n_task)
    outer, mid, inner = dims
    group = mid * inner
    tokens = inputs.shape[0]
    tasks, mats, rows, cols = task_vectors.shape
    heads = cols // HEAD
    pieces = math.gcd(tokens // 16, 3)
    hbm = pl.BlockSpec(memory_space=pl.ANY)
    vmem = pl.BlockSpec(memory_space=pltpu.VMEM)
    dma = pltpu.SemaphoreType.DMA

    def pair(count):
        return [dma((count,)), dma((count,))]

    attended, mean_entropy, coef_grad = pl.pallas_call(
        functools.partial(whole_kernel, dims, n_tensor, pieces),
        out_shape=(
            jax.ShapeDtypeStruct(queries.shape, BF16),
            jax.ShapeDtypeStruct((1, 1), F32),
            jax.ShapeDtypeStruct((mats, tasks), F32),
        ),
        in_specs=[hbm, vmem, hbm, hbm, hbm, hbm],
        out_specs=(vmem, vmem, vmem),
        scratch_shapes=[
            pltpu.VMEM((outer, tokens, group * rows), BF16),
            pltpu.VMEM((group, mats, rows, cols), BF16),
            pltpu.VMEM(task_vectors.shape, BF16),
            pltpu.VMEM(base_weights.shape, BF16),
            pltpu.VMEM((mats, tokens, cols), F32),
            pltpu.VMEM((mats, tokens, cols), F32),
            pltpu.VMEM((outer, mats, tokens, cols), BF16),
            pltpu.VMEM((outer, mats, tokens, cols), BF16),
            pltpu.VMEM((mats, tokens, cols), BF16),
            pltpu.VMEM((n_task, tokens, rows), BF16),
            pltpu.VMEM((mats, tokens, cols), BF16),
            pltpu.VMEM((heads, tokens, GROUP * tokens), F32),
            pltpu.VMEM((heads, GROUP * tokens, HEAD), F32),
            pltpu.VMEM((heads, GROUP * tokens, HEAD), F32),
            pltpu.VMEM((n_tensor, 8, tokens), F32),
            pltpu.VMEM((mats, n_task, tokens, cols), BF16),
            pltpu.VMEM((mats, rows, cols), F32),
            pltpu.VMEM((n_task, 8, 128), F32),
            pltpu.VMEM((n_tensor, 8, 128), F32),
            dma((2,)),
            pltpu.SMEM((mats, *scale_exps.shape[2:], tasks), jnp.int32), pltpu.SMEM((mats, tasks), F32),
            dma((2 + mats,)), dma((pieces * outer,)),
            *pair(outer * pieces),
            *pair(pieces * outer * n_tensor),
            *pair(mats * group),
            *pair(pieces * n_task),
            *pair(outer * pieces * mats),
            *pair(n_tensor),
            *pair(mats * n_task),
            *pair(n_task),
            *pair(n_tensor),
        ],
        compiler_params=pltpu.CompilerParams(
            collective_id=0, has_side_effects=True, vmem_limit_bytes=VMEM_BYTES
        ),
        name="whole",
    )(inputs, queries, task_vectors, base_weights, scale_exps.transpose(1, 2, 3, 0), coefs.T)
    return (attended, mean_entropy[0, 0], coef_grad.T)


def solution(mesh):
    return jax.shard_map(
        local,
        mesh=mesh,
        in_specs=(
            P("task", None),
            P("task", "tensor"),
            P(None, None, "task", "tensor"),
            P(None, "task", "tensor"),
            P(None, None, "task", "tensor"),
            P(),
        ),
        out_specs=(P("task", "tensor"), P(), P()),
        check_vma=False,
    )
```
